512 devices in a mesh: sky: 128 (over z, x, core), band: 4 (over y).
Axes of the slice: x: 4, y: 4, z: 16, core: 2. Of those that a mesh axis runs over, the one named last changes fastest.
Arguments:
- tiles: bfloat16 [4, 8192, 32, 256], P('band', 'sky'), may hold values from -6 to 6
- coefs: bfloat16 [4, 8192, 5], P('band', 'sky'), may hold values from -3 to 3
- tile_patch: int32 [4, 8192, 1], P('band', 'sky'), may hold values from 0 to 127; in each aligned block of 64 rows (0 to 63, 64 to 127, ..., all dimensions but the last counted through in order) at most 2 rows name the same one
- tile_offset: int32 [4, 8192], P('band', 'sky'), may hold values from 0 to 32
- weight_index: int32 [4, 8192], P('band', 'sky'), may hold values from 0 to 15
- weight_table: bfloat16 [4, 16], P('band'), may hold values from 0.5 to 2
- taps_rows: bfloat16 [4, 5, 41], P('band'), may hold values from -1 to 1
- taps_cols: bfloat16 [4, 5, 41], P('band'), may hold values from -1 to 1
- gains: float32 [4], P('band'), may hold values from 0.5 to 2
- profiles: bfloat16 [4, 8192, 256], P('band', 'sky'), may hold values from -0.375 to 0.375
- source_patch: int32 [4, 8192, 1], P('band', 'sky'), may hold values from 0 to 127; in each aligned block of 64 rows (0 to 63, 64 to 127, ..., all dimensions but the last counted through in order) at most 2 rows name the same one
- source_row: int32 [4, 8192], P('band', 'sky'), may hold values from 0 to 63
Outputs:
- coadded: float32 [4, 8192, 256], P('band', 'sky')
- detection: float32 [8192, 256], P('sky')
- fluxes: float32 [4, 8192], P('band', 'sky')
The draws below stay inside these ranges and needn't reach their ends.
Inputs may be any that keep to these rules, and one draw needn't show every extreme that they name: `tile_patch`: in the strips of one device at most 2 go to one patch. `source_patch`: in the sources of one device at most 2 go to one patch.
All inputs are finite; a program needn't handle non-finite values.
Results may differ from the reference program's by a relative error of at most 0.0041.
Values may be sent and summed in bfloat16 or wider, within the bound.
No kernel may reach another device: no remote copies, remote signals or barrier semaphores. Data moves between devices by JAX's collectives and lax.ppermute only.
A program may use at most 64 MiB of HBM per device.

```python
import math
import jax
import jax.numpy as jnp
import numpy as np
from jax import lax

TDEV = 64
SDEV = 64
TH = 32
TW = 256
BASIS = 5
KTAPS = 41
VISITS = 16
PH = 64
NB = 4
PATCHES = 128
TILES = 8192
SRCS = 8192
CAP = 2
SCAP = 2
N_SKY = 128


def place_ends(entries, rng, least, top_value):
    dims = entries.shape
    place = [jax.random.randint(jax.random.fold_in(rng, axis), (), 0, dims[axis]) for axis in range(len(dims))]
    entries = entries.at[tuple(place)].set(least)
    longest = dims.index(max(dims))
    place[longest] = (place[longest] + 1) % dims[longest]
    return entries.at[tuple(place)].set(top_value)


def shard_levels(stream_key, dims, cuts, smallest, largest):
    loudness, own = 1.0, jax.random.fold_in(stream_key, 6)
    for position, shards_of in cuts:
        draws = jnp.exp(jax.random.uniform(jax.random.fold_in(own, position), (shards_of,), jnp.float32, smallest / len(cuts), largest / len(cuts)))
        loudness = loudness * jnp.repeat(draws, dims[position] // shards_of).reshape([-1 if axis == position else 1 for axis in range(len(dims))])
    return loudness


def assign_block(rng, own, number, rows, count, top, limit, lean):
    sequence = jax.random.permutation(rng, count)
    heavy_load, usual = portions_of(count, rows * top, limit, lean, True), portions_of(count, rows * top, limit, lean, False)
    places = jnp.arange(count)

    def named(lengths, offset_by):
        used = int((lengths > 0).sum())
        fixed = max(1, used // 4)
        moved = fixed + (places - fixed + offset_by * (used - fixed)) % max(1, count - fixed)
        return jnp.zeros((count,), jnp.int32).at[sequence[jnp.where(places < fixed, places, moved)]].set(jnp.asarray(lengths, jnp.int32))

    lengths = jnp.where(number % 4 == 0, named(heavy_load, number // 4), named(usual, number - number // 4 - 1))
    mixed = jax.random.permutation(jax.random.fold_in(own, 3), count)
    giver, receiver = mixed[0:count // 2 * 2:2], mixed[1:count // 2 * 2:2]
    slack = jnp.minimum(lengths[giver] - 1, limit - lengths[receiver]) // 2
    slack = jnp.where((giver == sequence[0]) | (receiver == sequence[0]) | (lengths[receiver] == 0), 0, jnp.maximum(slack, 0))
    moved = jax.random.randint(jax.random.fold_in(own, 4), (count // 2,), 0, 1 << 20) % (slack + 1)
    lengths = lengths.at[giver].add(-moved).at[receiver].add(moved)
    labels = jnp.searchsorted(jnp.cumsum(lengths), jnp.arange(rows * top), side="right").astype(jnp.int32)
    table = labels.reshape(top, rows).T
    table = table[jax.random.permutation(jax.random.fold_in(own, 1), rows)]
    offset_by = jax.random.randint(jax.random.fold_in(own, 2), (rows, 1), 0, top)
    return jnp.take_along_axis(table, (jnp.arange(top)[None, :] + offset_by) % top, axis=1)


def portions_of(number_of, total, most, skew, full):
    portions = [(1 << 20) // math.isqrt(standing ** skew) + 1 for standing in range(1, number_of + 1)]
    largest = most if full else min(most, max(-(-total // number_of), total * portions[0] // sum(portions)))
    least = 1 if total - largest >= number_of - 1 else 0
    given, spare = [largest] + [least] * (number_of - 1), total - largest - least * (number_of - 1)
    while spare > 0:
        free = [i for i in range(1, number_of) if given[i] < largest] or [i for i in range(1, number_of) if given[i] < most]
        whole, remaining = sum([portions[i] for i in free]), spare
        for i in free:
            extra = min(most - given[i], max(1, remaining * portions[i] // whole), spare)
            given[i] = given[i] + extra
            spare = spare - extra
    return np.array(given)


def bell_draw(own_key, dims, deviation, limit, cuts=(), kind=jnp.bfloat16):
    drawn = jax.random.normal(own_key, dims, jnp.float32) * deviation
    if len(cuts) > 0:
        drawn = shard_levels(own_key, dims, cuts, -0.22, 0.18) * drawn
    return jnp.clip(drawn, min=-limit, max=limit).astype(kind)


def setup_inputs(seed: int = 0) -> dict:
    arg_keys = jax.random.split(jax.random.key(seed), 13)
    tiles = bell_draw(arg_keys[0], (NB, TILES, TH, TW), 1.0, 6.0, ((0, 4), (1, 128)))
    coefs = bell_draw(arg_keys[1], (NB, TILES, BASIS), 0.5, 3.0, ((0, 4), (1, 128)))
    tile_patch_keys = jax.random.split(jax.random.fold_in(arg_keys[2], 1), NB * TILES // TDEV)
    tile_patch_turns = jax.random.permutation(jax.random.fold_in(arg_keys[2], 3), NB * TILES // TDEV)
    tile_patch = jax.vmap(lambda own, number: assign_block(jax.random.fold_in(arg_keys[2], 2), own, number, TDEV, PATCHES, 1, CAP, 2))(tile_patch_keys, tile_patch_turns).reshape((NB, TILES, 1))
    tile_offset = place_ends(jax.random.randint(arg_keys[3], (NB, TILES), 0, TH + 1), jax.random.fold_in(arg_keys[3], 1), 0, TH).astype(jnp.int32)
    weight_index = place_ends(jax.random.randint(arg_keys[4], (NB, TILES), 0, VISITS), jax.random.fold_in(arg_keys[4], 1), 0, VISITS - 1).astype(jnp.int32)
    weight_table = jnp.clip(jnp.exp(math.log(2.0) - 1.3862944 * jax.random.uniform(arg_keys[5], (NB, VISITS), jnp.float32) ** shard_levels(arg_keys[5], (NB, VISITS), ((0, 4),), -0.2, 0.2)), 0.5, 2.0).astype(jnp.bfloat16)
    taps_rows = bell_draw(arg_keys[6], (NB, BASIS, KTAPS), KTAPS ** -0.5, 1.0, ((0, 4),))
    taps_cols = bell_draw(arg_keys[7], (NB, BASIS, KTAPS), KTAPS ** -0.5, 1.0, ((0, 4),))
    gains = jnp.clip(jnp.exp(math.log(2.0) - 1.3862944 * jax.random.uniform(arg_keys[8], (NB,), jnp.float32) ** shard_levels(arg_keys[8], (NB,), ((0, 4),), -0.2, 0.2)), 0.5, 2.0)
    profiles = bell_draw(arg_keys[9], (NB, SRCS, TW), TW ** -0.5, 0.375, ((0, 4), (1, 128)))
    source_patch_keys = jax.random.split(jax.random.fold_in(arg_keys[10], 1), NB * SRCS // SDEV)
    source_patch_turns = jax.random.permutation(jax.random.fold_in(arg_keys[10], 3), NB * SRCS // SDEV)
    source_patch = jax.vmap(lambda own, number: assign_block(jax.random.fold_in(arg_keys[10], 2), own, number, SDEV, PATCHES, 1, SCAP, 2))(source_patch_keys, source_patch_turns).reshape((NB, SRCS, 1))
    source_row = place_ends(jax.random.randint(arg_keys[11], (NB, SRCS), 0, PH), jax.random.fold_in(arg_keys[11], 1), 0, PH - 1).astype(jnp.int32)
    return {"tiles": tiles, "coefs": coefs, "tile_patch": tile_patch, "tile_offset": tile_offset, "weight_index": weight_index, "weight_table": weight_table, "taps_rows": taps_rows, "taps_cols": taps_cols, "gains": gains, "profiles": profiles, "source_patch": source_patch, "source_row": source_row}


def band_matrix(taps, size):
    tap_total = taps.shape[1]
    half_width = (tap_total - 1) // 2
    row_ids = jnp.arange(size, dtype=jnp.int32)[:, None]
    col_ids = jnp.arange(size, dtype=jnp.int32)[None, :]
    offset_lag = row_ids - col_ids + half_width
    inside = (offset_lag >= 0) & (offset_lag < tap_total)
    picked = jnp.take(taps, jnp.clip(offset_lag, 0, tap_total - 1), axis=1)
    return jnp.where(inside[None], picked, jnp.zeros((), taps.dtype))


def match_tiles(pixels, weights_k, vertical, horizontal):
    across = jnp.einsum("nij,kjl->nkil", pixels.astype(jnp.float32), horizontal.astype(jnp.float32))
    across = (across * weights_k.astype(jnp.float32)[:, :, None, None]).astype(jnp.bfloat16)
    matched = jnp.einsum("kia,nkal->nil", vertical.astype(jnp.float32), across.astype(jnp.float32))
    return matched.astype(jnp.bfloat16)


def reference(tiles, coefs, tile_patch, tile_offset, weight_index, weight_table, taps_rows, taps_cols, gains, profiles, source_patch, source_row):
    coadd_list = []
    for band_id in range(NB):
        vertical = band_matrix(taps_rows[band_id], TH)
        horizontal = jnp.transpose(band_matrix(taps_cols[band_id], TW), (0, 2, 1))

        def one_block(pair):
            return match_tiles(pair[0], pair[1], vertical, horizontal)

        matched = lax.map(one_block, (tiles[band_id].reshape(N_SKY, TDEV, TH, TW), coefs[band_id].reshape(N_SKY, TDEV, BASIS)))
        matched = matched.reshape(TILES, TH, TW)
        weight = weight_table[band_id][weight_index[band_id]].astype(jnp.float32)
        row_index = (tile_patch[band_id, :, 0] * PH + tile_offset[band_id]).astype(jnp.int32)[:, None] + jnp.arange(TH, dtype=jnp.int32)[None, :]
        numerator = jnp.zeros((PATCHES * PH, TW), jnp.float32).at[row_index].add(weight[:, None, None] * matched.astype(jnp.float32))
        coverage = jnp.zeros((PATCHES * PH,), jnp.float32).at[row_index].add(jnp.broadcast_to(weight[:, None], row_index.shape))
        coadd_list.append(numerator / jnp.maximum(coverage, 1.0)[:, None])
    coadded = jnp.stack(coadd_list)
    detection = jnp.sum(gains.astype(jnp.float32)[:, None, None] * coadded, axis=0)
    flux_list = []
    for band_id in range(NB):
        rows_read = (source_patch[band_id, :, 0] * PH + source_row[band_id]).astype(jnp.int32)
        picked = jnp.take(detection, rows_read, axis=0)
        flux_list.append(jnp.sum(profiles[band_id].astype(jnp.float32) * picked, axis=1))
    return coadded, detection, jnp.stack(flux_list)
```

```python
import jax
import jax.numpy as jnp
from jax import lax
from jax.experimental import pallas as pl
from jax.experimental.pallas import tpu as pltpu
from jax.sharding import PartitionSpec as P

F32 = jnp.float32
BF16 = jnp.bfloat16
I32 = jnp.int32
NT = (((1,), (1,)), ((), ()))


def iota(shape, dim):
    return lax.broadcasted_iota(I32, shape, dim)


def as_column(row):
    n = row.shape[1]
    eye = iota((n, n), 0) == iota((n, n), 1)
    return jnp.sum(jnp.where(eye, jnp.broadcast_to(row, (n, n)), jnp.zeros_like(row)), axis=1, keepdims=True)


def ranks(patch):
    n = patch.shape[1]
    column = as_column(patch)
    same = (column == patch) & (iota((n, n), 0) < iota((n, n), 1))
    return jnp.sum(same.astype(I32), axis=0, keepdims=True)


def one_hots(patch, total):
    rank = ranks(patch)
    named = iota((total, patch.shape[1]), 0) == patch
    return named & (rank == 0), named & (rank == 1)


def payload_kernel(tp_ref, to_ref, wi_ref, wt_ref, prof_ref, sp_ref, sr_ref, meta_ref, out_ref, stage):
    total = out_ref.shape[0]
    n = tp_ref.shape[1]
    patch = tp_ref[...]
    offset = to_ref[...]
    visits = wt_ref.shape[1]
    visit_hot = iota((visits, n), 0) == wi_ref[...]
    table = as_column(wt_ref[...].astype(F32))
    weight = jnp.sum(jnp.where(visit_hot, table, 0.0), axis=0, keepdims=True)
    meta_ref[0:1, :] = patch
    meta_ref[1:2, :] = offset
    meta_ref[2:3, :] = (weight * 256.0).astype(I32)
    lane = iota((n, 128), 1)
    off_col = as_column(offset.astype(F32))
    w_col = as_column(weight)
    tile_info = jnp.where(lane == 1, off_col, jnp.where(lane == 2, w_col, 0.0)).astype(BF16)
    row_col = as_column(sr_ref[...].astype(F32))
    src_info = jnp.where(lane == 0, row_col, 0.0).astype(BF16)
    tile_hots = one_hots(patch, total)
    src_hots = one_hots(sp_ref[...], total)
    prof = prof_ref[...]
    for s in range(2):
        hot = src_hots[s].astype(F32).astype(BF16)
        sent = jnp.dot(hot, prof, preferred_element_type=F32)
        stage[:, 2 * s, :] = sent[:, :128]
        stage[:, 2 * s + 1, :] = sent[:, 128:]
        thot = tile_hots[s].astype(F32).astype(BF16)
        stage[:, 4 + s, :] = jnp.dot(hot, src_info, preferred_element_type=F32) + jnp.dot(
            thot, tile_info, preferred_element_type=F32
        )
        stage[:, 6 + s, :] = jnp.zeros((total, 128), F32)
    out_ref[...] = stage[...].astype(BF16)


def match_kernel(tiles_ref, coef_ref, tr_ref, tc_ref, out_ref, taps_s, v_s, u_s, ce_s, a_s):
    basis, tap_total = tc_ref.shape
    half = (tap_total - 1) // 2
    cols = tiles_ref.shape[1]
    th = out_ref.shape[1]
    group = 256 // th
    taps_s[...] = jnp.zeros(taps_s.shape, F32)
    taps_s[0:basis, 0:tap_total] = tc_ref[...].astype(F32)
    taps_s[8 : 8 + basis, 0:tap_total] = tr_ref[...].astype(F32)
    taps_s[...] = pltpu.roll(taps_s[...], cols - half, 1)
    lag = iota((cols, cols), 1) - iota((cols, cols), 0)
    inside = (lag >= -half) & (lag <= half)
    for k in range(basis):
        rows = jnp.broadcast_to(taps_s[k : k + 1, :], (cols, cols))
        rolled = pltpu.roll(rows, 0, 1, stride=1, stride_axis=0)
        v_s[k] = jnp.where(inside, rolled, 0.0).astype(BF16)
    parts = []
    for k in range(basis):
        rows = jnp.broadcast_to(taps_s[8 + k : 9 + k, :], (th, cols))
        rolled = pltpu.roll(rows, 0, 1, stride=1, stride_axis=0)
        parts.append(jnp.where(inside[0:th, :], rolled, 0.0)[:, 0:128])
    parts.append(jnp.zeros((256 - basis * th, 128), F32))
    vertical = jnp.concatenate(parts, axis=0).T
    u_s[...] = vertical[0:th, 0 : basis * th].astype(BF16)
    n = coef_ref.shape[1]
    spread = (iota((n * th, n), 0) // th == iota((n * th, n), 1)).astype(F32).astype(BF16)
    ce_s[:, 0:basis] = lax.dot_general(spread, coef_ref[...], NT, preferred_element_type=F32)

    def one_group(g, carry):
        start = pl.multiple_of(g * 256, 256)
        pixels = tiles_ref[pl.ds(start, 256), :]
        coef = ce_s[pl.ds(start, 256), :]
        for k in range(basis):
            across = jnp.dot(pixels, v_s[k], preferred_element_type=F32)
            across = (across * coef[:, k : k + 1]).astype(BF16)
            a_s[:, k * th : (k + 1) * th, :] = across.reshape(group, th, cols)
        for t in range(group):
            done = jnp.dot(u_s[...], a_s[t], preferred_element_type=F32)
            out_ref[g * group + t] = done.astype(BF16)
        return carry

    lax.fori_loop(0, n // group, one_group, 0)


def place_kernel(core_ref, mine_ref, other_ref, m_ref, o_ref, out_ref, canvas):
    core = core_ref[0]
    th = m_ref.shape[1]
    canvas[...] = jnp.zeros(canvas.shape, F32)
    zs = canvas.shape[0] // 4

    for meta, strips in ((mine_ref, m_ref), (other_ref, o_ref)):

        def one_strip(t, carry, meta=meta, strips=strips):
            patch = meta[0, t]

            @pl.when((patch & 1) == core)
            def _():
                q = patch >> 1
                at = (q & 3) * zs + (q >> 2)
                off = meta[1, t]
                w = meta[2, t].astype(F32) * (1.0 / 256.0)
                strip = strips[t].astype(F32) * w
                for h in range(canvas.shape[1]):
                    canvas[at, h, pl.ds(off, th), :] += strip[:, h * 128 : (h + 1) * 128]

            return carry

        lax.fori_loop(0, strips.shape[0], one_strip, 0)
    for h in range(canvas.shape[1]):
        out_ref[:, :, h * 128 : (h + 1) * 128] = canvas[:, h].astype(BF16)


def coadd_kernel(parts_ref, got_ref, gain_ref, out_ref, scaled_ref):
    rows, cols = out_ref.shape
    numerator = jnp.sum(parts_ref[...].astype(F32), axis=0)
    info = got_ref[...].astype(F32)
    total = got_ref.shape[0]
    ids = iota((total, rows), 1).astype(F32)
    coverage = jnp.zeros((1, rows), F32)
    for s in range(2):
        details = info[:, 4 + s, :]
        off, w = details[:, 1:2], details[:, 2:3]
        covered = (ids >= off) & (ids < off + rows // 2)
        coverage = coverage + jnp.sum(jnp.where(covered, w, 0.0), axis=0, keepdims=True)
    column = as_column(jnp.maximum(coverage, 1.0))
    coadded = numerator / column
    out_ref[...] = coadded
    scaled_ref[...] = jnp.broadcast_to((gain_ref[0] * coadded)[None], scaled_ref.shape)


def measure_kernel(bands_ref, got_ref, det_ref, out_ref):
    detection = jnp.sum(bands_ref[...], axis=0)
    det_ref[...] = detection
    info = got_ref[...].astype(F32)
    total = got_ref.shape[0]
    rows = det_ref.shape[0]
    ids = iota((total, rows), 1).astype(F32)
    results = []
    for s in range(2):
        prof = jnp.concatenate([info[:, 2 * s, :], info[:, 2 * s + 1, :]], axis=1)
        row = info[:, 4 + s, 0:1]
        each = lax.dot_general(prof, detection, NT, precision=lax.Precision.HIGHEST, preferred_element_type=F32)
        results.append(jnp.sum(jnp.where(ids == row, each, 0.0), axis=1, keepdims=True))
    lane = iota(out_ref.shape, 1)
    out_ref[...] = jnp.where(lane == 0, results[0], results[1])


def pick_kernel(back_ref, sp_ref, out_ref):
    hots = one_hots(sp_ref[...], back_ref.shape[0])
    back = back_ref[...]
    out_ref[...] = jnp.sum(
        jnp.where(hots[0], back[:, 0:1], 0.0) + jnp.where(hots[1], back[:, 1:2], 0.0), axis=0, keepdims=True
    )


VM = pl.BlockSpec(memory_space=pltpu.VMEM)
SM = pl.BlockSpec(memory_space=pltpu.SMEM)
SDS = jax.ShapeDtypeStruct


def exchange(value, groups=None, axis="sky"):
    return lax.all_to_all(value, axis, split_axis=0, concat_axis=0, tiled=True, axis_index_groups=groups)


def per_device(
    tiles, coefs, tile_patch, tile_offset, weight_index, weight_table,
    taps_rows, taps_cols, gains, profiles, source_patch, source_row,
):
    sky = lax.axis_size("sky")
    band = lax.axis_size("band")
    _, n, th, cols = tiles.shape
    rows = 2 * th
    basis = coefs.shape[2]
    zs = sky // 8
    x_groups = [[(z * 4 + x) * 2 + c for x in range(4)] for z in range(zs) for c in range(2)]
    z_groups = [[(z * 4 + x) * 2 + c for z in range(zs)] for x in range(4) for c in range(2)]
    partners = [(i, i ^ 1) for i in range(sky)]
    core = (lax.axis_index("sky") % 2).astype(I32)[None]

    meta, payload = pl.pallas_call(
        payload_kernel,
        out_shape=(SDS((3, n), I32), SDS((sky, 8, 128), BF16)),
        in_specs=[VM] * 7,
        out_specs=(VM, VM),
        scratch_shapes=[pltpu.VMEM((sky, 8, 128), F32)],
        name="payload",
    )(
        tile_patch[:, :, 0], tile_offset, weight_index, weight_table,
        profiles[0], source_patch[:, :, 0], source_row,
    )
    other_meta = lax.ppermute(meta, "sky", partners)

    matched = pl.pallas_call(
        match_kernel,
        out_shape=SDS((n, th, cols), BF16),
        in_specs=[VM] * 4,
        out_specs=VM,
        scratch_shapes=[
            pltpu.VMEM((16, cols), F32),
            pltpu.VMEM((basis, cols, cols), BF16),
            pltpu.VMEM((th, basis * th), BF16),
            pltpu.VMEM((n * th, 8), F32),
            pltpu.VMEM((256 // th, basis * th, cols), BF16),
        ],
        name="match",
    )(tiles.reshape(n * th, cols), coefs[0].T, taps_rows[0], taps_cols[0])
    other = lax.ppermute(matched, "sky", partners)

    canvas = pl.pallas_call(
        place_kernel,
        out_shape=SDS((sky // 2, rows, cols), BF16),
        in_specs=[SM, SM, SM, VM, VM],
        out_specs=VM,
        scratch_shapes=[pltpu.VMEM((sky // 2, cols // 128, rows, 128), F32)],
        name="place",
    )(core, meta, other_meta, matched, other)

    along_x = exchange(canvas, x_groups).reshape(4, zs, rows, cols)
    got = exchange(payload)
    partial = jnp.sum(along_x.astype(F32), axis=0).astype(BF16)
    along_z = exchange(partial, z_groups)

    coadded, scaled = pl.pallas_call(
        coadd_kernel,
        out_shape=(SDS((rows, cols), F32), SDS((band, rows, cols), F32)),
        in_specs=[VM, VM, SM],
        out_specs=(VM, VM),
        name="coadd",
    )(along_z, got, gains)
    bands = exchange(scaled, None, "band")
    detection, measured = pl.pallas_call(
        measure_kernel,
        out_shape=(SDS((rows, cols), F32), SDS((sky, 2), F32)),
        in_specs=[VM, VM],
        out_specs=(VM, VM),
        name="measured",
    )(bands, got)
    returned = exchange(measured)
    fluxes = pl.pallas_call(
        pick_kernel,
        out_shape=SDS((1, profiles.shape[1]), F32),
        in_specs=[VM, VM],
        out_specs=VM,
        name="pick",
    )(returned, source_patch[:, :, 0])
    return coadded[None], detection, fluxes


def solution(mesh):
    return jax.shard_map(
        per_device,
        mesh=mesh,
        in_specs=(
            P("band", "sky", None, None),
            P("band", "sky", None),
            P("band", "sky", None),
            P("band", "sky"),
            P("band", "sky"),
            P("band", None),
            P("band", None, None),
            P("band", None, None),
            P("band"),
            P("band", "sky", None),
            P("band", "sky", None),
            P("band", "sky"),
        ),
        out_specs=(P("band", "sky", None), P("sky", None), P("band", "sky")),
        check_vma=False,
    )
```

```python
import jax
import jax.numpy as jnp
from jax import lax
from jax.experimental import pallas as pl
from jax.experimental.pallas import tpu as pltpu
from jax.sharding import PartitionSpec as P

F32 = jnp.float32
BF16 = jnp.bfloat16
I32 = jnp.int32
NT = (((1,), (1,)), ((), ()))
TN = (((0,), (0,)), ((), ()))


def iota(shape, dim):
    return lax.broadcasted_iota(I32, shape, dim)


def as_column(row):
    n = row.shape[1]
    eye = iota((n, n), 0) == iota((n, n), 1)
    return jnp.sum(jnp.where(eye, jnp.broadcast_to(row, (n, n)), jnp.zeros_like(row)), axis=1, keepdims=True)


def ranks(patch):
    n = patch.shape[1]
    column = as_column(patch)
    same = (column == patch) & (iota((n, n), 0) < iota((n, n), 1))
    return jnp.sum(same.astype(I32), axis=0, keepdims=True)


def write_details(out_ref, tp_ref, to_ref, wi_ref, wt_ref, sp_ref, sr_ref):
    n = tp_ref.shape[1]
    visits = wt_ref.shape[1]
    table = as_column(wt_ref[...].astype(F32))
    weight = jnp.sum(jnp.where(iota((visits, n), 0) == wi_ref[...], table, 0.0), axis=0, keepdims=True)
    rows = [tp_ref[...].astype(F32), to_ref[...].astype(F32), weight]
    rows += [sp_ref[...].astype(F32), sr_ref[...].astype(F32), ranks(sp_ref[...]).astype(F32)]
    rows.append(jnp.zeros((8 - len(rows), n), F32))
    block = jnp.concatenate(rows, axis=0).astype(BF16)
    out_ref[out_ref.shape[0] - 1, 0:8, 0:128] = jnp.concatenate([block, jnp.zeros((8, 128 - n), BF16)], axis=1)


def match_kernel(
    tiles_ref, coef_ref, tr_ref, tc_ref, tp_ref, to_ref, wi_ref, wt_ref, sp_ref, sr_ref,
    out_ref, taps_s, v_s, u_s, ce_s, a_s,
):
    write_details(out_ref, tp_ref, to_ref, wi_ref, wt_ref, sp_ref, sr_ref)
    basis, tap_total = tc_ref.shape
    half = (tap_total - 1) // 2
    cols = tiles_ref.shape[1]
    th = out_ref.shape[1]
    group = 256 // th
    taps_s[...] = jnp.zeros(taps_s.shape, F32)
    taps_s[0:basis, 0:tap_total] = tc_ref[...].astype(F32)
    taps_s[8 : 8 + basis, 0:tap_total] = tr_ref[...].astype(F32)
    taps_s[...] = pltpu.roll(taps_s[...], cols - half, 1)
    lag = iota((cols, cols), 1) - iota((cols, cols), 0)
    inside = (lag >= -half) & (lag <= half)
    for k in range(basis):
        rows = jnp.broadcast_to(taps_s[k : k + 1, :], (cols, cols))
        rolled = pltpu.roll(rows, 0, 1, stride=1, stride_axis=0)
        v_s[k] = jnp.where(inside, rolled, 0.0).astype(BF16)
    parts = []
    for k in range(basis):
        rows = jnp.broadcast_to(taps_s[8 + k : 9 + k, :], (th, cols))
        rolled = pltpu.roll(rows, 0, 1, stride=1, stride_axis=0)
        parts.append(jnp.where(inside[0:th, :], rolled, 0.0)[:, 0:128])
    parts.append(jnp.zeros((256 - basis * th, 128), F32))
    vertical = jnp.concatenate(parts, axis=0).T
    u_s[...] = vertical[0:th, 0 : basis * th].astype(BF16)
    n = coef_ref.shape[1]
    spread = (iota((n * th, n), 0) // th == iota((n * th, n), 1)).astype(F32).astype(BF16)
    ce_s[:, 0:basis] = lax.dot_general(spread, coef_ref[...], NT, preferred_element_type=F32)

    def one_group(g, carry):
        start = pl.multiple_of(g * 256, 256)
        pixels = tiles_ref[pl.ds(start, 256), :]
        coef = ce_s[pl.ds(start, 256), :]
        for k in range(basis):
            across = jnp.dot(pixels, v_s[k], preferred_element_type=F32)
            across = (across * coef[:, k : k + 1]).astype(BF16)
            a_s[:, k * th : (k + 1) * th, :] = across.reshape(group, th, cols)
        for t in range(group):
            done = jnp.dot(u_s[...], a_s[t], preferred_element_type=F32)
            out_ref[g * group + t] = done.astype(BF16)
        return carry

    lax.fori_loop(0, n // group, one_group, 0)


def place_kernel(here_ref, m_ref, o_ref, out_ref, canvas, words_s, words, sem):
    core = here_ref[0]
    first = here_ref[1]
    n = m_ref.shape[0] - 1
    th = m_ref.shape[1]
    rows = 2 * th
    for i, strips in enumerate((m_ref, o_ref)):
        details = strips[n, 0:8, 0:128].astype(F32)
        scale = jnp.where(iota(details.shape, 0) == 2, 256.0, 1.0)
        words_s[i] = (details * scale).astype(I32)
    copy = pltpu.make_async_copy(words_s, words, sem)
    copy.start()
    canvas[...] = jnp.zeros(canvas.shape, F32)
    copy.wait()
    depth = canvas.shape[0] // 8
    lane = iota((1, 128), 1)

    def place_of(patch):
        q = patch >> 1
        x, z = q & 3, q >> 2
        return ((z & 1) * 4 + x) * depth + (z >> 1)

    for i, strips in enumerate((m_ref, o_ref)):
        slots = first + 2 * (core if i == 0 else 1 - core)

        def one(t, carry, i=i, strips=strips, slots=slots):
            patch = words[i, 0, t]

            @pl.when((patch & 1) == core)
            def _():
                at = place_of(patch)
                off = words[i, 1, t]
                w = words[i, 2, t].astype(F32) * (1.0 / 256.0)
                strip = strips[t].astype(F32) * w
                for h in range(canvas.shape[1]):
                    canvas[at, h, pl.ds(off, th), :] += strip[:, h * 128 : (h + 1) * 128]
                covered = (lane >= off) & (lane < off + th)
                canvas[at, 0, rows : rows + 1, :] += jnp.where(covered, w, 0.0)

            patch_s = words[i, 3, t]

            @pl.when((patch_s & 1) == core)
            def _():
                at = place_of(patch_s)
                slot = slots + words[i, 5, t]
                value = words[i, 4, t].astype(F32)
                for h in range(canvas.shape[1]):
                    canvas[at, h, rows + 1 : rows + 2, :] += jnp.where(lane == slot - h * 128, value, 0.0)

            return carry

        lax.fori_loop(0, n, one, 0)
    for h in range(canvas.shape[1]):
        out_ref[:, :, h * 128 : (h + 1) * 128] = canvas[:, h].astype(BF16)


def add_kernel(parts_ref, out_ref):
    out_ref[...] = jnp.sum(parts_ref[...].astype(F32), axis=0).astype(BF16)


def coadd_kernel(parts_ref, gain_ref, out_ref, scaled_ref, asked_ref):
    rows, cols = out_ref.shape
    summed = jnp.sum(parts_ref[...].astype(F32), axis=0)
    column = as_column(jnp.maximum(summed[rows : rows + 1, 0:rows], 1.0))
    coadded = summed[0:rows] / column
    out_ref[...] = coadded
    scaled_ref[...] = jnp.broadcast_to((gain_ref[0] * coadded)[None], scaled_ref.shape)
    asked_ref[...] = summed[rows + 1 : rows + 2]


def detect_kernel(bands_ref, asked_ref, det_ref, rows_ref):
    detection = jnp.sum(bands_ref[...], axis=0)
    det_ref[...] = detection
    rows = det_ref.shape[0]
    ids = iota((rows, asked_ref.shape[1]), 0).astype(F32)
    hot = (ids == asked_ref[...]).astype(F32).astype(BF16)
    picked = lax.dot_general(hot, detection.astype(BF16), TN, preferred_element_type=F32)
    rows_ref[...] = picked.astype(BF16)


def flux_kernel(rows_ref, prof_ref, sp_ref, out_ref):
    patch = sp_ref[...]
    slot = 2 * patch + ranks(patch)
    each = lax.dot_general(rows_ref[...], prof_ref[...], NT, preferred_element_type=F32)
    wanted = iota(each.shape, 0) == slot
    out_ref[...] = jnp.sum(jnp.where(wanted, each, 0.0), axis=0, keepdims=True)


VM = pl.BlockSpec(memory_space=pltpu.VMEM)
SM = pl.BlockSpec(memory_space=pltpu.SMEM)
SDS = jax.ShapeDtypeStruct


def grant(mib):
    return pltpu.CompilerParams(vmem_limit_bytes=mib << 20)


def exchange(value, groups=None, axis="sky"):
    return lax.all_to_all(value, axis, split_axis=0, concat_axis=0, tiled=True, axis_index_groups=groups)


def per_device(
    tiles, coefs, tile_patch, tile_offset, weight_index, weight_table,
    taps_rows, taps_cols, gains, profiles, source_patch, source_row,
):
    sky = lax.axis_size("sky")
    band = lax.axis_size("band")
    _, n, th, cols = tiles.shape
    rows = 2 * th
    high = rows + 8
    basis = coefs.shape[2]
    depth = sky // 16
    sky_of = lambda z, x, c: (z * 4 + x) * 2 + c
    near = [[sky_of(2 * m + b, x, c) for b in range(2) for x in range(4)] for m in range(depth) for c in range(2)]
    far = [[sky_of(2 * m + b, x, c) for m in range(depth)] for b in range(2) for x in range(4) for c in range(2)]
    partners = [(i, i ^ 1) for i in range(sky)]
    me = lax.axis_index("sky").astype(I32)
    here = jnp.stack([me & 1, 2 * (me & ~1)])

    matched = pl.pallas_call(
        match_kernel,
        out_shape=SDS((n + 1, th, cols), BF16),
        in_specs=[VM] * 10,
        out_specs=VM,
        scratch_shapes=[
            pltpu.VMEM((16, cols), F32),
            pltpu.VMEM((basis, cols, cols), BF16),
            pltpu.VMEM((th, basis * th), BF16),
            pltpu.VMEM((n * th, 8), F32),
            pltpu.VMEM((256 // th, basis * th, cols), BF16),
        ],
        name="match",
        compiler_params=grant(10),
    )(
        tiles.reshape(n * th, cols), coefs[0].T, taps_rows[0], taps_cols[0],
        tile_patch[:, :, 0], tile_offset, weight_index, weight_table, source_patch[:, :, 0], source_row,
    )
    other = lax.ppermute(matched, "sky", partners)

    canvas = pl.pallas_call(
        place_kernel,
        out_shape=SDS((sky // 2, high, cols), BF16),
        in_specs=[SM, VM, VM],
        out_specs=VM,
        scratch_shapes=[
            pltpu.VMEM((sky // 2, cols // 128, high, 128), F32),
            pltpu.VMEM((2, 8, 128), I32),
            pltpu.SMEM((2, 8, 128), I32),
            pltpu.SemaphoreType.DMA,
        ],
        name="place",
        compiler_params=grant(14),
    )(here, matched, other)

    along_x = exchange(canvas, near).reshape(8, depth, high, cols)
    partial = pl.pallas_call(
        add_kernel, out_shape=SDS((depth, high, cols), BF16), in_specs=[VM], out_specs=VM, name="add",
        compiler_params=grant(8),
    )(along_x)
    along_z = exchange(partial, far)

    coadded, scaled, asked = pl.pallas_call(
        coadd_kernel,
        out_shape=(SDS((rows, cols), F32), SDS((band, rows, cols), F32), SDS((1, cols), F32)),
        in_specs=[VM, SM],
        out_specs=(VM, VM, VM),
        name="coadd",
        compiler_params=grant(4),
    )(along_z, gains)
    bands = exchange(scaled, None, "band")
    detection, picked = pl.pallas_call(
        detect_kernel,
        out_shape=(SDS((rows, cols), F32), SDS((2 * sky, cols), BF16)),
        in_specs=[VM, VM],
        out_specs=(VM, VM),
        name="detect",
        compiler_params=grant(4),
    )(bands, asked)
    returned = exchange(picked.reshape(sky, 2, cols)).reshape(2 * sky, cols)
    fluxes = pl.pallas_call(
        flux_kernel,
        out_shape=SDS((1, profiles.shape[1]), F32),
        in_specs=[VM, VM, VM],
        out_specs=VM,
        name="flux",
        compiler_params=grant(4),
    )(returned, profiles[0], source_patch[:, :, 0])
    return coadded[None], detection, fluxes


def solution(mesh):
    return jax.shard_map(
        per_device,
        mesh=mesh,
        in_specs=(
            P("band", "sky", None, None),
            P("band", "sky", None),
            P("band", "sky", None),
            P("band", "sky"),
            P("band", "sky"),
            P("band", None),
            P("band", None, None),
            P("band", None, None),
            P("band"),
            P("band", "sky", None),
            P("band", "sky", None),
            P("band", "sky"),
        ),
        out_specs=(P("band", "sky", None), P("sky", None), P("band", "sky")),
        check_vma=False,
    )
```

```python
import jax
import jax.numpy as jnp
from jax import lax
from jax.experimental import pallas as pl
from jax.experimental.pallas import tpu as pltpu
from jax.sharding import PartitionSpec as P

F32 = jnp.float32
BF16 = jnp.bfloat16
I32 = jnp.int32
NT = (((1,), (1,)), ((), ()))
TN = (((0,), (0,)), ((), ()))


def iota(shape, dim):
    return lax.broadcasted_iota(I32, shape, dim)


def as_column(row):
    n = row.shape[1]
    eye = iota((n, n), 0) == iota((n, n), 1)
    return jnp.sum(jnp.where(eye, jnp.broadcast_to(row, (n, n)), jnp.zeros_like(row)), axis=1, keepdims=True)


def ranks(patch):
    n = patch.shape[1]
    column = as_column(patch)
    same = (column == patch) & (iota((n, n), 0) < iota((n, n), 1))
    return jnp.sum(same.astype(I32), axis=0, keepdims=True)


def write_details(out_ref, tp_ref, to_ref, wi_ref, wt_ref, sp_ref, sr_ref):
    n = tp_ref.shape[1]
    visits = wt_ref.shape[1]
    table = as_column(wt_ref[...].astype(F32))
    weight = jnp.sum(jnp.where(iota((visits, n), 0) == wi_ref[...], table, 0.0), axis=0, keepdims=True)
    rows = [tp_ref[...].astype(F32), to_ref[...].astype(F32), weight]
    rows += [sp_ref[...].astype(F32), sr_ref[...].astype(F32), ranks(sp_ref[...]).astype(F32)]
    rows.append(jnp.zeros((8 - len(rows), n), F32))
    block = jnp.concatenate(rows, axis=0).astype(BF16)
    out_ref[out_ref.shape[0] - 1, 0:8, 0:128] = jnp.concatenate([block, jnp.zeros((8, 128 - n), BF16)], axis=1)


def match_kernel(*refs):
    sources, out_ref, scratch = refs[:10], refs[10], refs[11:]
    inner, held, sems = scratch[:5], scratch[5:15], scratch[15]
    copies = [pltpu.make_async_copy(src, dst, sems.at[i]) for i, (src, dst) in enumerate(zip(sources, held))]
    for copy in copies[::-1]:
        copy.start()
    for copy in copies[1:]:
        copy.wait()
    match_body(copies[0], *held, out_ref, *inner)


def match_body(
    tiles_copy, tiles_ref, coef_ref, tr_ref, tc_ref, tp_ref, to_ref, wi_ref, wt_ref, sp_ref, sr_ref,
    out_ref, taps_s, v_s, u_s, ce_s, a_s,
):
    write_details(out_ref, tp_ref, to_ref, wi_ref, wt_ref, sp_ref, sr_ref)
    basis, tap_total = tc_ref.shape
    half = (tap_total - 1) // 2
    cols = tiles_ref.shape[1]
    th = out_ref.shape[1]
    group = 256 // th
    taps_s[...] = jnp.zeros(taps_s.shape, F32)
    taps_s[0:basis, 0:tap_total] = tc_ref[...].astype(F32)
    taps_s[8 : 8 + basis, 0:tap_total] = tr_ref[...].astype(F32)
    taps_s[...] = pltpu.roll(taps_s[...], cols - half, 1)
    lag = iota((cols, cols), 1) - iota((cols, cols), 0)
    inside = (lag >= -half) & (lag <= half)
    for k in range(basis):
        rows = jnp.broadcast_to(taps_s[k : k + 1, :], (cols, cols))
        rolled = pltpu.roll(rows, 0, 1, stride=1, stride_axis=0)
        v_s[k] = jnp.where(inside, rolled, 0.0).astype(BF16)
    parts = []
    for k in range(basis):
        rows = jnp.broadcast_to(taps_s[8 + k : 9 + k, :], (th, cols))
        rolled = pltpu.roll(rows, 0, 1, stride=1, stride_axis=0)
        parts.append(jnp.where(inside[0:th, :], rolled, 0.0)[:, 0:128])
    parts.append(jnp.zeros((256 - basis * th, 128), F32))
    vertical = jnp.concatenate(parts, axis=0).T
    u_s[...] = vertical[0:th, 0 : basis * th].astype(BF16)
    n = coef_ref.shape[1]
    spread = (iota((n * th, n), 0) // th == iota((n * th, n), 1)).astype(F32).astype(BF16)
    ce_s[:, 0:basis] = lax.dot_general(spread, coef_ref[...], NT, preferred_element_type=F32)

    tiles_copy.wait()

    def one_group(g, carry):
        start = pl.multiple_of(g * 256, 256)
        pixels = tiles_ref[pl.ds(start, 256), :]
        coef = ce_s[pl.ds(start, 256), :]
        for k in range(basis):
            across = jnp.dot(pixels, v_s[k], preferred_element_type=F32)
            across = (across * coef[:, k : k + 1]).astype(BF16)
            a_s[:, k * th : (k + 1) * th, :] = across.reshape(group, th, cols)
        for t in range(group):
            done = jnp.dot(u_s[...], a_s[t], preferred_element_type=F32)
            out_ref[g * group + t] = done.astype(BF16)
        return carry

    lax.fori_loop(0, n // group, one_group, 0)


def place_kernel(me_ref, m_ref, o_ref, out_ref, canvas, words_s, words, sem):
    core = me_ref[0] & 1
    first = 2 * (me_ref[0] - core)
    n = m_ref.shape[0] - 1
    th = m_ref.shape[1]
    rows = 2 * th
    total = out_ref.shape[0]
    depth = total // 4

    def place_of(patch):
        q = patch >> 1
        x, z = q & 3, q >> 2
        return jnp.where((patch & 1) == core, x * depth + z, total)

    coverage = jnp.zeros((total, 128), F32)
    requests = jnp.zeros((total, 256), F32)
    lane = iota((n, 256), 1)
    copies = []
    for i, strips in enumerate((m_ref, o_ref)):
        details = strips[n, 0:8, 0:128].astype(F32)[:, 0:n]
        patch, offset, patch_s = (details[r : r + 1].astype(I32) for r in (0, 1, 3))
        weight, row_s, rank_s = (details[r : r + 1] for r in (2, 4, 5))
        at = place_of(patch)
        words_s[i, 0:1, 0:n] = at
        words_s[i, 1:2, 0:n] = offset
        words_s[i, 2:3, 0:n] = (weight * 256.0).astype(I32)
        copies.append(pltpu.make_async_copy(words_s.at[i], words.at[i], sem.at[i]))
        copies[-1].start()
        off_col = as_column(offset)
        covered = (lane >= off_col) & (lane < off_col + th)
        covers = jnp.where(covered, as_column(weight), 0.0)[:, 0:128].astype(BF16)
        here = (iota((total, n), 0) == at).astype(F32).astype(BF16)
        coverage += jnp.dot(here, covers, preferred_element_type=F32)
        slot = rank_s.astype(I32) + (first + 2 * (core if i == 0 else 1 - core))
        asks = jnp.where(lane == as_column(slot), as_column(row_s), 0.0).astype(BF16)
        there = (iota((total, n), 0) == place_of(patch_s)).astype(F32).astype(BF16)
        requests += jnp.dot(there, asks, preferred_element_type=F32)
    canvas[...] = jnp.zeros(canvas.shape, F32)
    canvas[0:total, 0, rows, :] = coverage
    for h in range(canvas.shape[1]):
        canvas[0:total, h, rows + 1, :] = requests[:, h * 128 : (h + 1) * 128]

    for i, strips in enumerate((m_ref, o_ref)):
        copies[i].wait()

        def one(t, carry, i=i, strips=strips):
            at = words[i, 0, t]
            off = words[i, 1, t]
            w = words[i, 2, t].astype(F32) * (1.0 / 256.0)
            strip = strips[t].astype(F32) * w
            for h in range(canvas.shape[1]):
                canvas[at, h, pl.ds(off, th), :] += strip[:, h * 128 : (h + 1) * 128]
            return carry

        lax.fori_loop(0, n, one, 0, unroll=4)
    for h in range(canvas.shape[1]):
        out_ref[:, :, h * 128 : (h + 1) * 128] = canvas[0:total, h].astype(BF16)


def add_kernel(parts_ref, out_ref):
    out_ref[...] = jnp.sum(parts_ref[...].astype(F32), axis=0).astype(BF16)


def coadd_kernel(parts_ref, gain_ref, out_ref, scaled_ref, asked_ref):
    rows, cols = out_ref.shape
    summed = jnp.sum(parts_ref[...].astype(F32), axis=0)
    column = as_column(jnp.maximum(summed[rows : rows + 1, 0:rows], 1.0))
    coadded = summed[0:rows] / column
    out_ref[...] = coadded
    scaled_ref[...] = jnp.broadcast_to((gain_ref[0] * coadded).astype(BF16)[None], scaled_ref.shape)
    asked_ref[...] = summed[rows + 1 : rows + 2]


def detect_kernel(bands_ref, asked_ref, det_ref, rows_ref):
    detection = jnp.sum(bands_ref[...].astype(F32), axis=0)
    det_ref[...] = detection
    rows = det_ref.shape[0]
    ids = iota((rows, asked_ref.shape[1]), 0).astype(F32)
    hot = (ids == asked_ref[...]).astype(F32).astype(BF16)
    picked = lax.dot_general(hot, detection.astype(BF16), TN, preferred_element_type=F32)
    rows_ref[...] = picked.astype(BF16)


def flux_kernel(rows_ref, prof_ref, sp_ref, out_ref):
    patch = sp_ref[...]
    slot = 2 * patch + ranks(patch)
    each = lax.dot_general(rows_ref[...], prof_ref[...], NT, preferred_element_type=F32)
    wanted = iota(each.shape, 0) == slot
    out_ref[...] = jnp.sum(jnp.where(wanted, each, 0.0), axis=0, keepdims=True)


VM = pl.BlockSpec(memory_space=pltpu.VMEM)
SM = pl.BlockSpec(memory_space=pltpu.SMEM)
SDS = jax.ShapeDtypeStruct


def grant(mib):
    return pltpu.CompilerParams(vmem_limit_bytes=mib << 20)


def exchange(value, groups=None, axis="sky"):
    return lax.all_to_all(value, axis, split_axis=0, concat_axis=0, tiled=True, axis_index_groups=groups)


def per_device(
    tiles, coefs, tile_patch, tile_offset, weight_index, weight_table,
    taps_rows, taps_cols, gains, profiles, source_patch, source_row,
):
    sky = lax.axis_size("sky")
    band = lax.axis_size("band")
    _, n, th, cols = tiles.shape
    rows = 2 * th
    high = rows + 8
    basis = coefs.shape[2]
    depth = sky // 8
    sky_of = lambda z, x, c: (z * 4 + x) * 2 + c
    near = [[sky_of(z, x, c) for x in range(4)] for z in range(depth) for c in range(2)]
    far = [[sky_of(z, x, c) for z in range(depth)] for x in range(4) for c in range(2)]
    partners = [(i, i ^ 1) for i in range(sky)]
    me = lax.axis_index("sky").astype(I32)[None]

    inputs = (
        tiles.reshape(n * th, cols), coefs[0].T, taps_rows[0], taps_cols[0],
        tile_patch[:, :, 0], tile_offset, weight_index, weight_table, source_patch[:, :, 0], source_row,
    )
    matched = pl.pallas_call(
        match_kernel,
        out_shape=SDS((n + 1, th, cols), BF16),
        in_specs=[pl.BlockSpec(memory_space=pltpu.HBM)] * 10,
        out_specs=VM,
        scratch_shapes=[
            pltpu.VMEM((16, cols), F32),
            pltpu.VMEM((basis, cols, cols), BF16),
            pltpu.VMEM((th, basis * th), BF16),
            pltpu.VMEM((n * th, 8), F32),
            pltpu.VMEM((256 // th, basis * th, cols), BF16),
        ]
        + [pltpu.VMEM(v.shape, v.dtype) for v in inputs]
        + [pltpu.SemaphoreType.DMA((len(inputs),))],
        name="match",
        compiler_params=grant(63),
    )(*inputs)
    other = lax.ppermute(matched, "sky", partners)

    canvas = pl.pallas_call(
        place_kernel,
        out_shape=SDS((sky // 2, high, cols), BF16),
        in_specs=[SM, VM, VM],
        out_specs=VM,
        scratch_shapes=[
            pltpu.VMEM((sky // 2 + 1, cols // 128, high, 128), F32),
            pltpu.VMEM((2, 8, 128), I32),
            pltpu.SMEM((2, 8, 128), I32),
            pltpu.SemaphoreType.DMA((2,)),
        ],
        name="place",
        compiler_params=grant(14),
    )(me, matched, other)

    along_x = exchange(canvas, near).reshape(4, depth, high, cols)
    partial = pl.pallas_call(
        add_kernel, out_shape=SDS((depth, high, cols), BF16), in_specs=[VM], out_specs=VM, name="add",
        compiler_params=grant(8),
    )(along_x)
    along_z = exchange(partial, far)

    coadded, scaled, asked = pl.pallas_call(
        coadd_kernel,
        out_shape=(SDS((rows, cols), F32), SDS((band, rows, cols), BF16), SDS((1, cols), F32)),
        in_specs=[VM, SM],
        out_specs=(VM, VM, VM),
        name="coadd",
        compiler_params=grant(4),
    )(along_z, gains)
    bands = exchange(scaled, None, "band")
    detection, picked = pl.pallas_call(
        detect_kernel,
        out_shape=(SDS((rows, cols), F32), SDS((2 * sky, cols), BF16)),
        in_specs=[VM, VM],
        out_specs=(VM, VM),
        name="detect",
        compiler_params=grant(4),
    )(bands, asked)
    returned = exchange(picked.reshape(sky, 2, cols)).reshape(2 * sky, cols)
    fluxes = pl.pallas_call(
        flux_kernel,
        out_shape=SDS((1, profiles.shape[1]), F32),
        in_specs=[VM, VM, VM],
        out_specs=VM,
        name="flux",
        compiler_params=grant(4),
    )(returned, profiles[0], source_patch[:, :, 0])
    return coadded[None], detection, fluxes


def solution(mesh):
    return jax.shard_map(
        per_device,
        mesh=mesh,
        in_specs=(
            P("band", "sky", None, None),
            P("band", "sky", None),
            P("band", "sky", None),
            P("band", "sky"),
            P("band", "sky"),
            P("band", None),
            P("band", None, None),
            P("band", None, None),
            P("band"),
            P("band", "sky", None),
            P("band", "sky", None),
            P("band", "sky"),
        ),
        out_specs=(P("band", "sky", None), P("sky", None), P("band", "sky")),
        check_vma=False,
    )
```

```python
import jax
import jax.numpy as jnp
from jax import lax
from jax.experimental import pallas as pl
from jax.experimental.pallas import tpu as pltpu
from jax.sharding import PartitionSpec as P

F32 = jnp.float32
BF16 = jnp.bfloat16
I32 = jnp.int32
NT = (((1,), (1,)), ((), ()))
TN = (((0,), (0,)), ((), ()))


def iota(shape, dim):
    return lax.broadcasted_iota(I32, shape, dim)


def as_column(row):
    n = row.shape[1]
    eye = iota((n, n), 0) == iota((n, n), 1)
    return jnp.sum(jnp.where(eye, jnp.broadcast_to(row, (n, n)), jnp.zeros_like(row)), axis=1, keepdims=True)


def ranks(patch):
    n = patch.shape[1]
    column = as_column(patch)
    same = (column == patch) & (iota((n, n), 0) < iota((n, n), 1))
    return jnp.sum(same.astype(I32), axis=0, keepdims=True)


def write_details(out_ref, tp_ref, to_ref, wi_ref, wt_ref, sp_ref, sr_ref):
    n = tp_ref.shape[1]
    visits = wt_ref.shape[1]
    table = as_column(wt_ref[...].astype(F32))
    weight = jnp.sum(jnp.where(iota((visits, n), 0) == wi_ref[...], table, 0.0), axis=0, keepdims=True)
    rows = [tp_ref[...].astype(F32), to_ref[...].astype(F32), weight]
    rows += [sp_ref[...].astype(F32), sr_ref[...].astype(F32), ranks(sp_ref[...]).astype(F32)]
    rows.append(jnp.zeros((8 - len(rows), n), F32))
    block = jnp.concatenate(rows, axis=0).astype(BF16)
    out_ref[out_ref.shape[0] - 1, 0:8, 0:128] = jnp.concatenate([block, jnp.zeros((8, 128 - n), BF16)], axis=1)


def match_kernel(*refs):
    sources, out_ref, scratch = refs[:10], refs[10], refs[11:]
    inner, held, sems = scratch[:5], scratch[5:15], scratch[15]
    copies = [pltpu.make_async_copy(src, dst, sems.at[i]) for i, (src, dst) in enumerate(zip(sources, held))]
    for copy in copies[::-1]:
        copy.start()
    for copy in copies[1:]:
        copy.wait()
    match_body(copies[0], *held, out_ref, *inner)


def match_body(
    tiles_copy, tiles_ref, coef_ref, tr_ref, tc_ref, tp_ref, to_ref, wi_ref, wt_ref, sp_ref, sr_ref,
    out_ref, taps_s, v_s, u_s, ce_s, a_s,
):
    write_details(out_ref, tp_ref, to_ref, wi_ref, wt_ref, sp_ref, sr_ref)
    basis, tap_total = tc_ref.shape
    half = (tap_total - 1) // 2
    cols = tiles_ref.shape[1]
    th = out_ref.shape[1]
    group = 256 // th
    taps_s[...] = jnp.zeros(taps_s.shape, F32)
    taps_s[0:basis, 0:tap_total] = tc_ref[...].astype(F32)
    taps_s[8 : 8 + basis, 0:tap_total] = tr_ref[...].astype(F32)
    taps_s[...] = pltpu.roll(taps_s[...], cols - half, 1)
    lag = iota((cols, cols), 1) - iota((cols, cols), 0)
    inside = (lag >= -half) & (lag <= half)
    for k in range(basis):
        rows = jnp.broadcast_to(taps_s[k : k + 1, :], (cols, cols))
        rolled = pltpu.roll(rows, 0, 1, stride=1, stride_axis=0)
        v_s[k] = jnp.where(inside, rolled, 0.0).astype(BF16)
    parts = []
    for k in range(basis):
        rows = jnp.broadcast_to(taps_s[8 + k : 9 + k, :], (th, cols))
        rolled = pltpu.roll(rows, 0, 1, stride=1, stride_axis=0)
        parts.append(jnp.where(inside[0:th, :], rolled, 0.0)[:, 0:128])
    parts.append(jnp.zeros((256 - basis * th, 128), F32))
    vertical = jnp.concatenate(parts, axis=0).T
    u_s[...] = vertical[0:th, 0 : basis * th].astype(BF16)
    n = coef_ref.shape[1]
    spread = (iota((n * th, n), 0) // th == iota((n * th, n), 1)).astype(F32).astype(BF16)
    ce_s[:, 0:basis] = lax.dot_general(spread, coef_ref[...], NT, preferred_element_type=F32)

    tiles_copy.wait()

    def one_group(g, carry):
        start = pl.multiple_of(g * 256, 256)
        pixels = tiles_ref[pl.ds(start, 256), :]
        coef = ce_s[pl.ds(start, 256), :]
        for k in range(basis):
            across = jnp.dot(pixels, v_s[k], preferred_element_type=F32)
            across = (across * coef[:, k : k + 1]).astype(BF16)
            a_s[:, k * th : (k + 1) * th, :] = across.reshape(group, th, cols)
        for t in range(group):
            done = jnp.dot(u_s[...], a_s[t], preferred_element_type=F32)
            out_ref[g * group + t] = done.astype(BF16)
        return carry

    lax.fori_loop(0, n // group, one_group, 0)


def place_strips(me_ref, strips, sender, canvas, words_s, words, sem):
    core = me_ref[0] & 1
    first = 2 * (me_ref[0] - core)
    n = strips.shape[0] - 1
    th = strips.shape[1]
    rows = 2 * th
    total = canvas.shape[0] - 1
    depth = total // 8

    def place_of(patch):
        q = patch >> 1
        x, z = q & 3, q >> 2
        return jnp.where((patch & 1) == core, ((z & 1) * 4 + x) * depth + (z >> 1), total)

    lane = iota((n, 256), 1)
    details = strips[n, 0:8, 0:128].astype(F32)[:, 0:n]
    patch, offset, patch_s = (details[r : r + 1].astype(I32) for r in (0, 1, 3))
    weight, row_s, rank_s = (details[r : r + 1] for r in (2, 4, 5))
    at = place_of(patch)
    words_s[0:1, 0:n] = at
    words_s[1:2, 0:n] = offset
    words_s[2:3, 0:n] = (weight * 256.0).astype(I32)
    copy = pltpu.make_async_copy(words_s, words, sem)
    copy.start()
    off_col = as_column(offset)
    covered = (lane >= off_col) & (lane < off_col + th)
    covers = jnp.where(covered, as_column(weight), 0.0)[:, 0:128].astype(BF16)
    here = (iota((total, n), 0) == at).astype(F32).astype(BF16)
    coverage = jnp.dot(here, covers, preferred_element_type=F32)
    slot = rank_s.astype(I32) + (first + 2 * sender)
    asks = jnp.where(lane == as_column(slot), as_column(row_s), 0.0).astype(BF16)
    there = (iota((total, n), 0) == place_of(patch_s)).astype(F32).astype(BF16)
    requests = jnp.dot(there, asks, preferred_element_type=F32)

    def add_extras():
        for r, value in ((0, coverage), (1, requests[:, 0:128]), (2, requests[:, 128:256])):
            canvas[0:total, 2 * rows + r, :] = value

    def add_strips():
        copy.wait()

        def one(t, carry):
            at = words[0, t]
            off = words[1, t]
            w = words[2, t].astype(F32) * (1.0 / 256.0)
            strip = strips[t].astype(F32) * w
            for h in range(strip.shape[1] // 128):
                canvas[at, pl.ds(h * rows + off, th), :] += strip[:, h * 128 : (h + 1) * 128]
            return carry

        lax.fori_loop(0, n, one, 0, unroll=4)

    return add_extras, add_strips


def place_own_kernel(me_ref, m_ref, canvas, words_s, words, sem):
    add_extras, add_strips = place_strips(me_ref, m_ref, me_ref[0] & 1, canvas, words_s, words, sem)
    canvas[...] = jnp.zeros(canvas.shape, F32)
    add_extras()
    add_strips()


def place_other_kernel(me_ref, o_ref, own_ref, out_ref, canvas, words_s, words, sem):
    add_extras, add_strips = place_strips(me_ref, o_ref, 1 - (me_ref[0] & 1), canvas, words_s, words, sem)
    canvas[...] = jnp.zeros(canvas.shape, F32)
    add_extras()
    add_strips()
    total = out_ref.shape[0]
    out_ref[...] = (own_ref[0:total] + canvas[0:total]).astype(BF16)


def add_kernel(parts_ref, out_ref):
    out_ref[...] = jnp.sum(parts_ref[...].astype(F32), axis=0).astype(BF16)


def coadd_kernel(parts_ref, gain_ref, out_ref, scaled_ref, asked_ref):
    rows, cols = out_ref.shape
    summed = jnp.sum(parts_ref[...].astype(F32), axis=0)
    column = as_column(jnp.maximum(summed[2 * rows : 2 * rows + 1, 0:rows], 1.0))
    for h in range(cols // 128):
        part = slice(h * 128, (h + 1) * 128)
        coadded = summed[h * rows : (h + 1) * rows] / column
        out_ref[:, part] = coadded
        for b in range(scaled_ref.shape[0]):
            scaled_ref[b, :, part] = (gain_ref[0] * coadded).astype(BF16)
        asked_ref[:, part] = summed[2 * rows + 1 + h : 2 * rows + 2 + h]


def detect_kernel(bands_ref, asked_ref, det_ref, rows_ref):
    detection = jnp.sum(bands_ref[...].astype(F32), axis=0)
    det_ref[...] = detection
    rows = det_ref.shape[0]
    ids = iota((rows, asked_ref.shape[1]), 0).astype(F32)
    hot = (ids == asked_ref[...]).astype(F32).astype(BF16)
    picked = lax.dot_general(hot, detection.astype(BF16), TN, preferred_element_type=F32)
    rows_ref[...] = picked.astype(BF16)


def flux_kernel(rows_ref, prof_ref, sp_ref, out_ref):
    patch = sp_ref[...]
    slot = 2 * patch + ranks(patch)
    each = lax.dot_general(rows_ref[...], prof_ref[...], NT, preferred_element_type=F32)
    wanted = iota(each.shape, 0) == slot
    out_ref[...] = jnp.sum(jnp.where(wanted, each, 0.0), axis=0, keepdims=True)


VM = pl.BlockSpec(memory_space=pltpu.VMEM)
SM = pl.BlockSpec(memory_space=pltpu.SMEM)
SDS = jax.ShapeDtypeStruct


def grant(mib):
    return pltpu.CompilerParams(vmem_limit_bytes=mib << 20)


def exchange(value, groups=None, axis="sky"):
    return lax.all_to_all(value, axis, split_axis=0, concat_axis=0, tiled=True, axis_index_groups=groups)


def per_device(
    tiles, coefs, tile_patch, tile_offset, weight_index, weight_table,
    taps_rows, taps_cols, gains, profiles, source_patch, source_row,
):
    sky = lax.axis_size("sky")
    band = lax.axis_size("band")
    _, n, th, cols = tiles.shape
    rows = 2 * th
    high = rows * (cols // 128) + 8
    basis = coefs.shape[2]
    depth = sky // 16
    sky_of = lambda z, x, c: (z * 4 + x) * 2 + c
    near = [[sky_of(2 * m + b, x, c) for b in range(2) for x in range(4)] for m in range(depth) for c in range(2)]
    far = [[sky_of(2 * m + b, x, c) for m in range(depth)] for b in range(2) for x in range(4) for c in range(2)]
    partners = [(i, i ^ 1) for i in range(sky)]
    me = lax.axis_index("sky").astype(I32)[None]

    inputs = (
        tiles.reshape(n * th, cols), coefs[0].T, taps_rows[0], taps_cols[0],
        tile_patch[:, :, 0], tile_offset, weight_index, weight_table, source_patch[:, :, 0], source_row,
    )
    matched = pl.pallas_call(
        match_kernel,
        out_shape=SDS((n + 1, th, cols), BF16),
        in_specs=[pl.BlockSpec(memory_space=pltpu.HBM)] * 10,
        out_specs=VM,
        scratch_shapes=[
            pltpu.VMEM((16, cols), F32),
            pltpu.VMEM((basis, cols, cols), BF16),
            pltpu.VMEM((th, basis * th), BF16),
            pltpu.VMEM((n * th, 8), F32),
            pltpu.VMEM((256 // th, basis * th, cols), BF16),
        ]
        + [pltpu.VMEM(v.shape, v.dtype) for v in inputs]
        + [pltpu.SemaphoreType.DMA((len(inputs),))],
        name="match",
        compiler_params=grant(63),
    )(*inputs)
    other = lax.ppermute(matched, "sky", partners)

    place_scratch = [pltpu.VMEM((8, 128), I32), pltpu.SMEM((8, 128), I32), pltpu.SemaphoreType.DMA]
    own = pl.pallas_call(
        place_own_kernel,
        out_shape=SDS((sky // 2 + 1, high, 128), F32),
        in_specs=[SM, VM],
        out_specs=VM,
        scratch_shapes=place_scratch,
        name="place_own",
        compiler_params=grant(4),
    )(me, matched)
    canvas = pl.pallas_call(
        place_other_kernel,
        out_shape=SDS((sky // 2, high, 128), BF16),
        in_specs=[SM, VM, VM],
        out_specs=VM,
        scratch_shapes=[pltpu.VMEM(own.shape, F32)] + place_scratch,
        name="place_other",
        compiler_params=grant(10),
    )(me, other, own)

    along_x = exchange(canvas, near).reshape(8, depth, high, 128)
    partial = pl.pallas_call(
        add_kernel,
        out_shape=SDS((depth, high, 128), BF16),
        in_specs=[VM],
        out_specs=VM,
        name="add",
        compiler_params=grant(8),
    )(along_x)
    along_z = exchange(partial, far)

    coadded, scaled, asked = pl.pallas_call(
        coadd_kernel,
        out_shape=(SDS((rows, cols), F32), SDS((band, rows, cols), BF16), SDS((1, cols), F32)),
        in_specs=[VM, SM],
        out_specs=(VM, VM, VM),
        name="coadd",
        compiler_params=grant(4),
    )(along_z, gains)
    bands = exchange(scaled, None, "band")
    detection, picked = pl.pallas_call(
        detect_kernel,
        out_shape=(SDS((rows, cols), F32), SDS((2 * sky, cols), BF16)),
        in_specs=[VM, VM],
        out_specs=(VM, VM),
        name="detect",
        compiler_params=grant(4),
    )(bands, asked)
    returned = exchange(picked.reshape(sky, 2, cols)).reshape(2 * sky, cols)
    fluxes = pl.pallas_call(
        flux_kernel,
        out_shape=SDS((1, profiles.shape[1]), F32),
        in_specs=[VM, VM, VM],
        out_specs=VM,
        name="flux",
        compiler_params=grant(4),
    )(returned, profiles[0], source_patch[:, :, 0])
    return coadded[None], detection, fluxes


def solution(mesh):
    return jax.shard_map(
        per_device,
        mesh=mesh,
        in_specs=(
            P("band", "sky", None, None),
            P("band", "sky", None),
            P("band", "sky", None),
            P("band", "sky"),
            P("band", "sky"),
            P("band", None),
            P("band", None, None),
            P("band", None, None),
            P("band"),
            P("band", "sky", None),
            P("band", "sky", None),
            P("band", "sky"),
        ),
        out_specs=(P("band", "sky", None), P("sky", None), P("band", "sky")),
        check_vma=False,
    )
```

```python
import jax
import jax.numpy as jnp
from jax import lax
from jax.experimental import pallas as pl
from jax.experimental.pallas import tpu as pltpu
from jax.sharding import PartitionSpec as P

F32 = jnp.float32
BF16 = jnp.bfloat16
I32 = jnp.int32
NT = (((1,), (1,)), ((), ()))
TN = (((0,), (0,)), ((), ()))


def iota(shape, dim):
    return lax.broadcasted_iota(I32, shape, dim)


def as_column(row):
    n = row.shape[1]
    eye = iota((n, n), 0) == iota((n, n), 1)
    return jnp.sum(jnp.where(eye, jnp.broadcast_to(row, (n, n)), jnp.zeros_like(row)), axis=1, keepdims=True)


def ranks(patch):
    n = patch.shape[1]
    column = as_column(patch)
    same = (column == patch) & (iota((n, n), 0) < iota((n, n), 1))
    return jnp.sum(same.astype(I32), axis=0, keepdims=True)


def write_details(out_ref, tp_ref, to_ref, wi_ref, wt_ref, sp_ref, sr_ref):
    n = tp_ref.shape[1]
    visits = wt_ref.shape[1]
    table = as_column(wt_ref[...].astype(F32))
    weight = jnp.sum(jnp.where(iota((visits, n), 0) == wi_ref[...], table, 0.0), axis=0, keepdims=True)
    rows = [tp_ref[...].astype(F32), to_ref[...].astype(F32), weight]
    rows += [sp_ref[...].astype(F32), sr_ref[...].astype(F32), ranks(sp_ref[...]).astype(F32)]
    rows.append(jnp.zeros((8 - len(rows), n), F32))
    block = jnp.concatenate(rows, axis=0).astype(BF16)
    out_ref[out_ref.shape[0] - 1, 0:8, 0:128] = jnp.concatenate([block, jnp.zeros((8, 128 - n), BF16)], axis=1)


def match_kernel(*refs):
    sources, sent_ref, scratch = refs[:10], refs[10], refs[11:]
    taps_s, v_s, u_s, c_s, a_s, out_s = scratch[:6]
    held, sems, out_sems = scratch[6:16], scratch[16], scratch[17]
    tiles_ref, coef_ref, tr_ref, tc_ref = held[:4]
    copies = [pltpu.make_async_copy(src, dst, sems.at[i]) for i, (src, dst) in enumerate(zip(sources, held))]
    for i in (3, 2, 1, 0, 4, 5, 6, 7, 8, 9):
        copies[i].start()

    basis, tap_total = tc_ref.shape
    half = (tap_total - 1) // 2
    cols = tiles_ref.shape[1]
    th = out_s.shape[1]
    n = coef_ref.shape[1]
    group = 256 // th
    taps_s[...] = jnp.zeros(taps_s.shape, F32)
    lag = iota((cols, cols), 1) - iota((cols, cols), 0)
    inside = (lag >= -half) & (lag <= half)
    copies[3].wait()
    copies[2].wait()
    taps_s[0:basis, 0:tap_total] = tc_ref[...].astype(F32)
    taps_s[8 : 8 + basis, 0:tap_total] = tr_ref[...].astype(F32)
    taps_s[...] = pltpu.roll(taps_s[...], cols - half, 1)
    parts = []
    for k in range(basis):
        rows = jnp.broadcast_to(taps_s[8 + k : 9 + k, :], (th, cols))
        rolled = pltpu.roll(rows, 0, 1, stride=1, stride_axis=0)
        parts.append(jnp.where(inside[0:th, :], rolled, 0.0)[:, 0:128])
    parts.append(jnp.zeros((256 - basis * th, 128), F32))
    vertical = jnp.concatenate(parts, axis=0).T
    u_s[...] = vertical[0:th, 0 : basis * th].astype(BF16)
    for k in range(basis):
        rows = jnp.broadcast_to(taps_s[k : k + 1, :], (cols, cols))
        rolled = pltpu.roll(rows, 0, 1, stride=1, stride_axis=0)
        v_s[k] = jnp.where(inside, rolled, 0.0).astype(BF16)
    copies[1].wait()
    for k in range(basis):
        choose = (iota((basis, cols), 0) == k).astype(F32).astype(BF16)
        c_s[k] = lax.dot_general(coef_ref[...], choose, TN, preferred_element_type=F32)
    for i in range(4, 10):
        copies[i].wait()
    write_details(out_s, *held[4:])
    last = pltpu.make_async_copy(out_s.at[n], sent_ref.at[n], out_sems.at[n // group])
    last.start()
    copies[0].wait()

    def block(g):
        return pltpu.make_async_copy(
            out_s.at[pl.ds(g * group, group)], sent_ref.at[pl.ds(g * group, group)], out_sems.at[g]
        )

    def one_group(g, carry):
        start = pl.multiple_of(g * 256, 256)
        pixels = tiles_ref[pl.ds(start, 256), :]
        for k in range(basis):
            across = jnp.dot(pixels, v_s[k], preferred_element_type=F32)
            for t in range(group):
                coef = c_s[k, pl.ds(g * group + t, 1), :]
                part = across[t * th : (t + 1) * th] * coef
                a_s[g % 2, t, k * th : (k + 1) * th, :] = part.astype(BF16)
        for t in range(group):
            done = jnp.dot(u_s[...], a_s[g % 2, t], preferred_element_type=F32)
            out_s[g * group + t] = done.astype(BF16)
        block(g).start()
        return carry

    lax.fori_loop(0, n // group, one_group, 0, unroll=UNROLL)
    for g in range(n // group):
        block(g).wait()
    last.wait()


def place_strips(me_ref, strips, sender, canvas, words_s, words, sem):
    core = me_ref[0] & 1
    first = 2 * (me_ref[0] - core)
    n = strips.shape[0] - 1
    th = strips.shape[1]
    rows = 2 * th
    total = canvas.shape[0] - 1
    depth = total // 8

    def place_of(patch):
        q = patch >> 1
        x, z = q & 3, q >> 2
        return jnp.where((patch & 1) == core, ((z & 1) * 4 + x) * depth + (z >> 1), total)

    lane = iota((n, 256), 1)
    details = strips[n, 0:8, 0:128].astype(F32)[:, 0:n]
    patch, offset, patch_s = (details[r : r + 1].astype(I32) for r in (0, 1, 3))
    weight, row_s, rank_s = (details[r : r + 1] for r in (2, 4, 5))
    at = place_of(patch)
    words_s[0:1, 0:n] = at
    words_s[1:2, 0:n] = offset
    words_s[2:3, 0:n] = (weight * 256.0).astype(I32)
    copy = pltpu.make_async_copy(words_s, words, sem)
    copy.start()
    off_col = as_column(offset)
    covered = (lane >= off_col) & (lane < off_col + th)
    covers = jnp.where(covered, as_column(weight), 0.0)[:, 0:128].astype(BF16)
    here = (iota((total, n), 0) == at).astype(F32).astype(BF16)
    coverage = jnp.dot(here, covers, preferred_element_type=F32)
    slot = rank_s.astype(I32) + (first + 2 * sender)
    asks = jnp.where(lane == as_column(slot), as_column(row_s), 0.0).astype(BF16)
    there = (iota((total, n), 0) == place_of(patch_s)).astype(F32).astype(BF16)
    requests = jnp.dot(there, asks, preferred_element_type=F32)

    def add_extras():
        for r, value in ((0, coverage), (1, requests[:, 0:128]), (2, requests[:, 128:256])):
            canvas[0:total, 2 * rows + r, :] = value

    def add_strips():
        copy.wait()

        def one(t, carry):
            at = words[0, t]
            off = words[1, t]
            w = words[2, t].astype(F32) * (1.0 / 256.0)
            strip = strips[t].astype(F32) * w
            for h in range(strip.shape[1] // 128):
                canvas[at, pl.ds(h * rows + off, th), :] += strip[:, h * 128 : (h + 1) * 128]
            return carry

        lax.fori_loop(0, n, one, 0, unroll=4)

    return add_extras, add_strips


def place_own_kernel(me_ref, m_ref, canvas, words_s, words, sem):
    add_extras, add_strips = place_strips(me_ref, m_ref, me_ref[0] & 1, canvas, words_s, words, sem)
    canvas[...] = jnp.zeros(canvas.shape, F32)
    add_extras()
    add_strips()


def place_other_kernel(me_ref, o_ref, own_ref, out_ref, canvas, words_s, words, sem):
    add_extras, add_strips = place_strips(me_ref, o_ref, 1 - (me_ref[0] & 1), canvas, words_s, words, sem)
    canvas[...] = jnp.zeros(canvas.shape, F32)
    add_extras()
    add_strips()
    total = out_ref.shape[0]
    out_ref[...] = (own_ref[0:total] + canvas[0:total]).astype(BF16)


def add_kernel(parts_ref, out_ref):
    out_ref[...] = jnp.sum(parts_ref[...].astype(F32), axis=0).astype(BF16)


def coadd_kernel(parts_ref, gain_ref, out_ref, scaled_ref, asked_ref):
    rows, cols = out_ref.shape
    summed = jnp.sum(parts_ref[...].astype(F32), axis=0)
    column = as_column(jnp.maximum(summed[2 * rows : 2 * rows + 1, 0:rows], 1.0))
    for h in range(cols // 128):
        part = slice(h * 128, (h + 1) * 128)
        coadded = summed[h * rows : (h + 1) * rows] / column
        out_ref[:, part] = coadded
        for b in range(scaled_ref.shape[0]):
            scaled_ref[b, :, part] = (gain_ref[0] * coadded).astype(BF16)
        asked_ref[:, part] = summed[2 * rows + 1 + h : 2 * rows + 2 + h]


def detect_kernel(bands_ref, asked_ref, det_ref, rows_ref):
    detection = jnp.sum(bands_ref[...].astype(F32), axis=0)
    det_ref[...] = detection
    rows = det_ref.shape[0]
    ids = iota((rows, asked_ref.shape[1]), 0).astype(F32)
    hot = (ids == asked_ref[...]).astype(F32).astype(BF16)
    picked = lax.dot_general(hot, detection.astype(BF16), TN, preferred_element_type=F32)
    rows_ref[...] = picked.astype(BF16)


def flux_kernel(rows_ref, prof_ref, sp_ref, out_ref):
    patch = sp_ref[...]
    slot = 2 * patch + ranks(patch)
    each = lax.dot_general(rows_ref[...], prof_ref[...], NT, preferred_element_type=F32)
    wanted = iota(each.shape, 0) == slot
    out_ref[...] = jnp.sum(jnp.where(wanted, each, 0.0), axis=0, keepdims=True)


UNROLL = 2
VM = pl.BlockSpec(memory_space=pltpu.VMEM)
SM = pl.BlockSpec(memory_space=pltpu.SMEM)
SDS = jax.ShapeDtypeStruct


def grant(mib):
    return pltpu.CompilerParams(vmem_limit_bytes=mib << 20)


def exchange(value, groups=None, axis="sky"):
    return lax.all_to_all(value, axis, split_axis=0, concat_axis=0, tiled=True, axis_index_groups=groups)


def per_device(
    tiles, coefs, tile_patch, tile_offset, weight_index, weight_table,
    taps_rows, taps_cols, gains, profiles, source_patch, source_row,
):
    sky = lax.axis_size("sky")
    band = lax.axis_size("band")
    _, n, th, cols = tiles.shape
    rows = 2 * th
    high = rows * (cols // 128) + 8
    basis = coefs.shape[2]
    depth = sky // 16
    sky_of = lambda z, x, c: (z * 4 + x) * 2 + c
    near = [[sky_of(2 * m + b, x, c) for b in range(2) for x in range(4)] for m in range(depth) for c in range(2)]
    far = [[sky_of(2 * m + b, x, c) for m in range(depth)] for b in range(2) for x in range(4) for c in range(2)]
    partners = [(i, i ^ 1) for i in range(sky)]
    me = lax.axis_index("sky").astype(I32)[None]

    inputs = (
        tiles.reshape(n * th, cols), coefs[0].T, taps_rows[0], taps_cols[0],
        tile_patch[:, :, 0], tile_offset, weight_index, weight_table, source_patch[:, :, 0], source_row,
    )
    matched = pl.pallas_call(
        match_kernel,
        out_shape=SDS((n + 1, th, cols), BF16),
        in_specs=[pl.BlockSpec(memory_space=pltpu.HBM)] * 10,
        out_specs=pl.BlockSpec(memory_space=pltpu.HBM),
        scratch_shapes=[
            pltpu.VMEM((16, cols), F32),
            pltpu.VMEM((basis, cols, cols), BF16),
            pltpu.VMEM((th, basis * th), BF16),
            pltpu.VMEM((basis, n, cols), F32),
            pltpu.VMEM((2, 256 // th, basis * th, cols), BF16),
            pltpu.VMEM((n + 1, th, cols), BF16),
        ]
        + [pltpu.VMEM(v.shape, v.dtype) for v in inputs]
        + [pltpu.SemaphoreType.DMA((len(inputs),)), pltpu.SemaphoreType.DMA((n * th // 256 + 1,))],
        name="match",
        compiler_params=grant(63),
    )(*inputs)
    other = lax.ppermute(matched, "sky", partners)

    place_scratch = [pltpu.VMEM((8, 128), I32), pltpu.SMEM((8, 128), I32), pltpu.SemaphoreType.DMA]
    own = pl.pallas_call(
        place_own_kernel,
        out_shape=SDS((sky // 2 + 1, high, 128), F32),
        in_specs=[SM, VM],
        out_specs=VM,
        scratch_shapes=place_scratch,
        name="place_own",
        compiler_params=grant(4),
    )(me, matched)
    canvas = pl.pallas_call(
        place_other_kernel,
        out_shape=SDS((sky // 2, high, 128), BF16),
        in_specs=[SM, VM, VM],
        out_specs=VM,
        scratch_shapes=[pltpu.VMEM(own.shape, F32)] + place_scratch,
        name="place_other",
        compiler_params=grant(10),
    )(me, other, own)

    along_x = exchange(canvas, near).reshape(8, depth, high, 128)
    partial = pl.pallas_call(
        add_kernel,
        out_shape=SDS((depth, high, 128), BF16),
        in_specs=[VM],
        out_specs=VM,
        name="add",
        compiler_params=grant(8),
    )(along_x)
    along_z = exchange(partial, far)

    coadded, scaled, asked = pl.pallas_call(
        coadd_kernel,
        out_shape=(SDS((rows, cols), F32), SDS((band, rows, cols), BF16), SDS((1, cols), F32)),
        in_specs=[VM, SM],
        out_specs=(VM, VM, VM),
        name="coadd",
        compiler_params=grant(4),
    )(along_z, gains)
    bands = exchange(scaled, None, "band")
    detection, picked = pl.pallas_call(
        detect_kernel,
        out_shape=(SDS((rows, cols), F32), SDS((2 * sky, cols), BF16)),
        in_specs=[VM, VM],
        out_specs=(VM, VM),
        name="detect",
        compiler_params=grant(4),
    )(bands, asked)
    returned = exchange(picked.reshape(sky, 2, cols)).reshape(2 * sky, cols)
    fluxes = pl.pallas_call(
        flux_kernel,
        out_shape=SDS((1, profiles.shape[1]), F32),
        in_specs=[VM, VM, VM],
        out_specs=VM,
        name="flux",
        compiler_params=grant(4),
    )(returned, profiles[0], source_patch[:, :, 0])
    return coadded[None], detection, fluxes


def solution(mesh):
    return jax.shard_map(
        per_device,
        mesh=mesh,
        in_specs=(
            P("band", "sky", None, None),
            P("band", "sky", None),
            P("band", "sky", None),
            P("band", "sky"),
            P("band", "sky"),
            P("band", None),
            P("band", None, None),
            P("band", None, None),
            P("band"),
            P("band", "sky", None),
            P("band", "sky", None),
            P("band", "sky"),
        ),
        out_specs=(P("band", "sky", None), P("sky", None), P("band", "sky")),
        check_vma=False,
    )
```

```python
import jax
import jax.numpy as jnp
from jax import lax
from jax.experimental import pallas as pl
from jax.experimental.pallas import tpu as pltpu
from jax.sharding import PartitionSpec as P

F32 = jnp.float32
BF16 = jnp.bfloat16
I32 = jnp.int32
NT = (((1,), (1,)), ((), ()))
TN = (((0,), (0,)), ((), ()))


def iota(shape, dim):
    return lax.broadcasted_iota(I32, shape, dim)


def as_column(row):
    n = row.shape[1]
    eye = iota((n, n), 0) == iota((n, n), 1)
    return jnp.sum(jnp.where(eye, jnp.broadcast_to(row, (n, n)), jnp.zeros_like(row)), axis=1, keepdims=True)


def ranks(patch):
    n = patch.shape[1]
    column = as_column(patch)
    same = (column == patch) & (iota((n, n), 0) < iota((n, n), 1))
    return jnp.sum(same.astype(I32), axis=0, keepdims=True)


def write_details(out_ref, tp_ref, to_ref, wi_ref, wt_ref, sp_ref, sr_ref):
    n = tp_ref.shape[1]
    visits = wt_ref.shape[1]
    table = as_column(wt_ref[...].astype(F32))
    weight = jnp.sum(jnp.where(iota((visits, n), 0) == wi_ref[...], table, 0.0), axis=0, keepdims=True)
    rows = [tp_ref[...].astype(F32), to_ref[...].astype(F32), weight]
    rows += [sp_ref[...].astype(F32), sr_ref[...].astype(F32), ranks(sp_ref[...]).astype(F32)]
    rows.append(jnp.zeros((8 - len(rows), n), F32))
    block = jnp.concatenate(rows, axis=0).astype(BF16)
    out_ref[out_ref.shape[0] - 1, 0:8, 0:128] = jnp.concatenate([block, jnp.zeros((8, 128 - n), BF16)], axis=1)


def match_kernel(*refs):
    sources, sent_ref, scratch = refs[:10], refs[10], refs[11:]
    taps_s, v_s, u_s, c_s, a_s, out_s = scratch[:6]
    held, sems, out_sems = scratch[6:16], scratch[16], scratch[17]
    tiles_ref, coef_ref, tr_ref, tc_ref = held[:4]
    copies = [pltpu.make_async_copy(src, dst, sems.at[i]) for i, (src, dst) in enumerate(zip(sources, held))]
    for i in (3, 2, 1, 0, 4, 5, 6, 7, 8, 9):
        copies[i].start()

    basis, tap_total = tc_ref.shape
    half = (tap_total - 1) // 2
    cols = tiles_ref.shape[1]
    th = out_s.shape[1]
    n = coef_ref.shape[1]
    group = 256 // th
    taps_s[...] = jnp.zeros(taps_s.shape, F32)
    lag = iota((cols, cols), 1) - iota((cols, cols), 0)
    inside = (lag >= -half) & (lag <= half)
    copies[3].wait()
    copies[2].wait()
    taps_s[0:basis, 0:tap_total] = tc_ref[...].astype(F32)
    taps_s[8 : 8 + basis, 0:tap_total] = tr_ref[...].astype(F32)
    taps_s[...] = pltpu.roll(taps_s[...], cols - half, 1)
    parts = []
    for k in range(basis):
        rows = jnp.broadcast_to(taps_s[8 + k : 9 + k, :], (th, cols))
        rolled = pltpu.roll(rows, 0, 1, stride=1, stride_axis=0)
        parts.append(jnp.where(inside[0:th, :], rolled, 0.0)[:, 0:128])
    parts.append(jnp.zeros((256 - basis * th, 128), F32))
    vertical = jnp.concatenate(parts, axis=0).T
    u_s[...] = vertical[0:th, 0 : basis * th].astype(BF16)
    for k in range(basis):
        rows = jnp.broadcast_to(taps_s[k : k + 1, :], (cols, cols))
        rolled = pltpu.roll(rows, 0, 1, stride=1, stride_axis=0)
        v_s[k] = jnp.where(inside, rolled, 0.0).astype(BF16)
    copies[1].wait()
    for k in range(basis):
        choose = (iota((basis, cols), 0) == k).astype(F32).astype(BF16)
        c_s[k] = lax.dot_general(coef_ref[...], choose, TN, preferred_element_type=F32)
    for i in range(4, 10):
        copies[i].wait()
    write_details(out_s, *held[4:])
    last = pltpu.make_async_copy(out_s.at[n], sent_ref.at[n], out_sems.at[n // group])
    last.start()
    copies[0].wait()

    def block(g):
        return pltpu.make_async_copy(
            out_s.at[pl.ds(g * group, group)], sent_ref.at[pl.ds(g * group, group)], out_sems.at[g]
        )

    def one_group(g, carry):
        start = pl.multiple_of(g * 256, 256)
        pixels = tiles_ref[pl.ds(start, 256), :]
        for k in range(basis):
            across = jnp.dot(pixels, v_s[k], preferred_element_type=F32)
            for t in range(group):
                coef = c_s[k, pl.ds(g * group + t, 1), :]
                part = across[t * th : (t + 1) * th] * coef
                a_s[g % 2, t, k * th : (k + 1) * th, :] = part.astype(BF16)
        for t in range(group):
            done = jnp.dot(u_s[...], a_s[g % 2, t], preferred_element_type=F32)
            out_s[g * group + t] = done.astype(BF16)
        block(g).start()
        return carry

    lax.fori_loop(0, n // group, one_group, 0, unroll=UNROLL)
    for g in range(n // group):
        block(g).wait()
    last.wait()


def place_strips(me_ref, strips, sender, canvas, words_s, words, sem):
    core = me_ref[0] & 1
    first = 2 * (me_ref[0] - core)
    n = strips.shape[0] - 1
    th = strips.shape[1]
    rows = 2 * th
    total = canvas.shape[0] - 1
    depth = total // 8

    def place_of(patch):
        q = patch >> 1
        x, z = (q + core) & 3, ((q >> 2) + core) & (2 * depth - 1)
        pair = x >> 1
        member = (z & 1) * 2 + ((x ^ pair) & 1)
        return jnp.where((patch & 1) == core, (member * 2 + pair) * depth + (z >> 1), total)

    lane = iota((n, 256), 1)
    details = strips[n, 0:8, 0:128].astype(F32)[:, 0:n]
    patch, offset, patch_s = (details[r : r + 1].astype(I32) for r in (0, 1, 3))
    weight, row_s, rank_s = (details[r : r + 1] for r in (2, 4, 5))
    at = place_of(patch)
    words_s[0:1, 0:n] = at
    words_s[1:2, 0:n] = offset
    words_s[2:3, 0:n] = (weight * 256.0).astype(I32)
    copy = pltpu.make_async_copy(words_s, words, sem)
    copy.start()
    off_col = as_column(offset)
    covered = (lane >= off_col) & (lane < off_col + th)
    covers = jnp.where(covered, as_column(weight), 0.0)[:, 0:128].astype(BF16)
    here = (iota((total, n), 0) == at).astype(F32).astype(BF16)
    coverage = jnp.dot(here, covers, preferred_element_type=F32)
    slot = rank_s.astype(I32) + (first + 2 * sender)
    asks = jnp.where(lane == as_column(slot), as_column(row_s), 0.0).astype(BF16)
    there = (iota((total, n), 0) == place_of(patch_s)).astype(F32).astype(BF16)
    requests = jnp.dot(there, asks, preferred_element_type=F32)

    def add_extras():
        for r, value in ((0, coverage), (1, requests[:, 0:128]), (2, requests[:, 128:256])):
            canvas[0:total, 2 * rows + r, :] = value

    def add_strips():
        copy.wait()

        def one(t, carry):
            at = words[0, t]
            off = words[1, t]
            w = words[2, t].astype(F32) * (1.0 / 256.0)
            strip = strips[t].astype(F32) * w
            for h in range(strip.shape[1] // 128):
                canvas[at, pl.ds(h * rows + off, th), :] += strip[:, h * 128 : (h + 1) * 128]
            return carry

        lax.fori_loop(0, n, one, 0, unroll=4)

    return add_extras, add_strips


def place_own_kernel(me_ref, m_ref, canvas, words_s, words, sem):
    add_extras, add_strips = place_strips(me_ref, m_ref, me_ref[0] & 1, canvas, words_s, words, sem)
    canvas[...] = jnp.zeros(canvas.shape, F32)
    add_extras()
    add_strips()


def place_other_kernel(me_ref, o_ref, own_ref, out_ref, canvas, words_s, words, sem):
    add_extras, add_strips = place_strips(me_ref, o_ref, 1 - (me_ref[0] & 1), canvas, words_s, words, sem)
    canvas[...] = jnp.zeros(canvas.shape, F32)
    add_extras()
    add_strips()
    total = out_ref.shape[0]
    out_ref[...] = (own_ref[0:total] + canvas[0:total]).astype(BF16)


def split_kernel(me_ref, parts_ref, keep_ref, send_ref):
    pair = (((me_ref[0] >> 1) + (me_ref[0] & 1)) & 3) >> 1
    members = range(parts_ref.shape[0])
    send_ref[...] = sum(parts_ref[s, 1 - pair].astype(F32) for s in members).astype(BF16)
    keep_ref[...] = sum(parts_ref[s, pair].astype(F32) for s in members)


def add_kernel(keep_ref, got_ref, out_ref):
    out_ref[...] = (keep_ref[...] + got_ref[...].astype(F32)).astype(BF16)


def coadd_kernel(parts_ref, gain_ref, out_ref, scaled_ref, asked_ref):
    rows, cols = out_ref.shape
    summed = jnp.sum(parts_ref[...].astype(F32), axis=0)
    column = as_column(jnp.maximum(summed[2 * rows : 2 * rows + 1, 0:rows], 1.0))
    for h in range(cols // 128):
        part = slice(h * 128, (h + 1) * 128)
        coadded = summed[h * rows : (h + 1) * rows] / column
        out_ref[:, part] = coadded
        for b in range(scaled_ref.shape[0]):
            scaled_ref[b, :, part] = (gain_ref[0] * coadded).astype(BF16)
        asked_ref[:, part] = summed[2 * rows + 1 + h : 2 * rows + 2 + h]


def detect_kernel(bands_ref, asked_ref, det_ref, rows_ref):
    detection = jnp.sum(bands_ref[...].astype(F32), axis=0)
    det_ref[...] = detection
    rows = det_ref.shape[0]
    ids = iota((rows, asked_ref.shape[1]), 0).astype(F32)
    hot = (ids == asked_ref[...]).astype(F32).astype(BF16)
    picked = lax.dot_general(hot, detection.astype(BF16), TN, preferred_element_type=F32)
    rows_ref[...] = picked.astype(BF16)


def flux_kernel(rows_ref, prof_ref, sp_ref, out_ref):
    patch = sp_ref[...]
    slot = 2 * patch + ranks(patch)
    each = lax.dot_general(rows_ref[...], prof_ref[...], NT, preferred_element_type=F32)
    wanted = iota(each.shape, 0) == slot
    out_ref[...] = jnp.sum(jnp.where(wanted, each, 0.0), axis=0, keepdims=True)


UNROLL = 2
VM = pl.BlockSpec(memory_space=pltpu.VMEM)
SM = pl.BlockSpec(memory_space=pltpu.SMEM)
SDS = jax.ShapeDtypeStruct


def grant(mib):
    return pltpu.CompilerParams(vmem_limit_bytes=mib << 20)


def exchange(value, groups=None, axis="sky"):
    return lax.all_to_all(value, axis, split_axis=0, concat_axis=0, tiled=True, axis_index_groups=groups)


def per_device(
    tiles, coefs, tile_patch, tile_offset, weight_index, weight_table,
    taps_rows, taps_cols, gains, profiles, source_patch, source_row,
):
    sky = lax.axis_size("sky")
    band = lax.axis_size("band")
    _, n, th, cols = tiles.shape
    rows = 2 * th
    high = rows * (cols // 128) + 8
    basis = coefs.shape[2]
    depth = sky // 16
    sky_of = lambda z, x, c: (z * 4 + x) * 2 + c
    device = lambda c, x, z: sky_of((z - c) % (2 * depth), (x - c) % 4, c)
    spots = [(c, m) for c in range(2) for m in range(depth)]
    near = [
        [device(c, (3 * g) ^ e, 2 * m + b) for b in range(2) for e in range(2)] for c, m in spots for g in range(2)
    ]
    cross = [(device(c, x, z), device(c, 3 - x, z)) for c in range(2) for x in range(4) for z in range(2 * depth)]
    far = [
        [device(c, x, 2 * m + b) for m in range(depth)] for c in range(2) for b in range(2) for x in range(4)
    ]
    partners = [(i, i ^ 1) for i in range(sky)]
    me = lax.axis_index("sky").astype(I32)[None]

    inputs = (
        tiles.reshape(n * th, cols), coefs[0].T, taps_rows[0], taps_cols[0],
        tile_patch[:, :, 0], tile_offset, weight_index, weight_table, source_patch[:, :, 0], source_row,
    )
    matched = pl.pallas_call(
        match_kernel,
        out_shape=SDS((n + 1, th, cols), BF16),
        in_specs=[pl.BlockSpec(memory_space=pltpu.HBM)] * 10,
        out_specs=pl.BlockSpec(memory_space=pltpu.HBM),
        scratch_shapes=[
            pltpu.VMEM((16, cols), F32),
            pltpu.VMEM((basis, cols, cols), BF16),
            pltpu.VMEM((th, basis * th), BF16),
            pltpu.VMEM((basis, n, cols), F32),
            pltpu.VMEM((2, 256 // th, basis * th, cols), BF16),
            pltpu.VMEM((n + 1, th, cols), BF16),
        ]
        + [pltpu.VMEM(v.shape, v.dtype) for v in inputs]
        + [pltpu.SemaphoreType.DMA((len(inputs),)), pltpu.SemaphoreType.DMA((n * th // 256 + 1,))],
        name="match",
        compiler_params=grant(63),
    )(*inputs)
    other = lax.ppermute(matched, "sky", partners)

    place_scratch = [pltpu.VMEM((8, 128), I32), pltpu.SMEM((8, 128), I32), pltpu.SemaphoreType.DMA]
    own = pl.pallas_call(
        place_own_kernel,
        out_shape=SDS((sky // 2 + 1, high, 128), F32),
        in_specs=[SM, VM],
        out_specs=VM,
        scratch_shapes=place_scratch,
        name="place_own",
        compiler_params=grant(4),
    )(me, matched)
    canvas = pl.pallas_call(
        place_other_kernel,
        out_shape=SDS((sky // 2, high, 128), BF16),
        in_specs=[SM, VM, VM],
        out_specs=VM,
        scratch_shapes=[pltpu.VMEM(own.shape, F32)] + place_scratch,
        name="place_other",
        compiler_params=grant(10),
    )(me, other, own)

    along_x = exchange(canvas, near).reshape(4, 2, depth, high, 128)
    keep, send = pl.pallas_call(
        split_kernel,
        out_shape=(SDS((depth, high, 128), F32), SDS((depth, high, 128), BF16)),
        in_specs=[SM, VM],
        out_specs=(VM, VM),
        name="split",
        compiler_params=grant(8),
    )(me, along_x)
    partial = pl.pallas_call(
        add_kernel,
        out_shape=SDS((depth, high, 128), BF16),
        in_specs=[VM, VM],
        out_specs=VM,
        name="add",
        compiler_params=grant(8),
    )(keep, lax.ppermute(send, "sky", cross))
    along_z = exchange(partial, far)

    coadded, scaled, asked = pl.pallas_call(
        coadd_kernel,
        out_shape=(SDS((rows, cols), F32), SDS((band, rows, cols), BF16), SDS((1, cols), F32)),
        in_specs=[VM, SM],
        out_specs=(VM, VM, VM),
        name="coadd",
        compiler_params=grant(4),
    )(along_z, gains)
    bands = exchange(scaled, None, "band")
    detection, picked = pl.pallas_call(
        detect_kernel,
        out_shape=(SDS((rows, cols), F32), SDS((2 * sky, cols), BF16)),
        in_specs=[VM, VM],
        out_specs=(VM, VM),
        name="detect",
        compiler_params=grant(4),
    )(bands, asked)
    returned = exchange(picked.reshape(sky, 2, cols)).reshape(2 * sky, cols)
    fluxes = pl.pallas_call(
        flux_kernel,
        out_shape=SDS((1, profiles.shape[1]), F32),
        in_specs=[VM, VM, VM],
        out_specs=VM,
        name="flux",
        compiler_params=grant(4),
    )(returned, profiles[0], source_patch[:, :, 0])
    return coadded[None], detection, fluxes


def solution(mesh):
    return jax.shard_map(
        per_device,
        mesh=mesh,
        in_specs=(
            P("band", "sky", None, None),
            P("band", "sky", None),
            P("band", "sky", None),
            P("band", "sky"),
            P("band", "sky"),
            P("band", None),
            P("band", None, None),
            P("band", None, None),
            P("band"),
            P("band", "sky", None),
            P("band", "sky", None),
            P("band", "sky"),
        ),
        out_specs=(P("band", "sky", None), P("sky", None), P("band", "sky")),
        check_vma=False,
    )
```

```python
import jax
import jax.numpy as jnp
from jax import lax
from jax.experimental import pallas as pl
from jax.experimental.pallas import tpu as pltpu
from jax.sharding import PartitionSpec as P

F32 = jnp.float32
BF16 = jnp.bfloat16
I32 = jnp.int32
NT = (((1,), (1,)), ((), ()))
TN = (((0,), (0,)), ((), ()))


def iota(shape, dim):
    return lax.broadcasted_iota(I32, shape, dim)


def as_column(row):
    n = row.shape[1]
    eye = iota((n, n), 0) == iota((n, n), 1)
    return jnp.sum(jnp.where(eye, jnp.broadcast_to(row, (n, n)), jnp.zeros_like(row)), axis=1, keepdims=True)


def ranks(patch):
    n = patch.shape[1]
    column = as_column(patch)
    same = (column == patch) & (iota((n, n), 0) < iota((n, n), 1))
    return jnp.sum(same.astype(I32), axis=0, keepdims=True)


def write_details(out_ref, tp_ref, to_ref, wi_ref, wt_ref, sp_ref, sr_ref):
    n = tp_ref.shape[1]
    visits = wt_ref.shape[1]
    table = as_column(wt_ref[...].astype(F32))
    weight = jnp.sum(jnp.where(iota((visits, n), 0) == wi_ref[...], table, 0.0), axis=0, keepdims=True)
    rows = [tp_ref[...].astype(F32), to_ref[...].astype(F32), weight]
    rows += [sp_ref[...].astype(F32), sr_ref[...].astype(F32), ranks(sp_ref[...]).astype(F32)]
    rows.append(jnp.zeros((8 - len(rows), n), F32))
    block = jnp.concatenate(rows, axis=0).astype(BF16)
    out_ref[out_ref.shape[0] - 1, 0:8, 0:128] = jnp.concatenate([block, jnp.zeros((8, 128 - n), BF16)], axis=1)


def match_kernel(*refs):
    sources, sent_ref, scratch = refs[:10], refs[10], refs[11:]
    taps_s, v_s, u_s, c_s, a_s, out_s = scratch[:6]
    held, sems, out_sems = scratch[6:16], scratch[16], scratch[17]
    tiles_ref, coef_ref, tr_ref, tc_ref = held[:4]
    copies = [pltpu.make_async_copy(src, dst, sems.at[i]) for i, (src, dst) in enumerate(zip(sources, held))]
    for i in (3, 2, 1, 0, 4, 5, 6, 7, 8, 9):
        copies[i].start()

    basis, tap_total = tc_ref.shape
    half = (tap_total - 1) // 2
    cols = tiles_ref.shape[1]
    th = out_s.shape[1]
    n = coef_ref.shape[1]
    group = 256 // th
    taps_s[...] = jnp.zeros(taps_s.shape, F32)
    lag = iota((cols, cols), 1) - iota((cols, cols), 0)
    inside = (lag >= -half) & (lag <= half)
    copies[3].wait()
    copies[2].wait()
    taps_s[0:basis, 0:tap_total] = tc_ref[...].astype(F32)
    taps_s[8 : 8 + basis, 0:tap_total] = tr_ref[...].astype(F32)
    taps_s[...] = pltpu.roll(taps_s[...], cols - half, 1)
    parts = []
    for k in range(basis):
        rows = jnp.broadcast_to(taps_s[8 + k : 9 + k, :], (th, cols))
        rolled = pltpu.roll(rows, 0, 1, stride=1, stride_axis=0)
        parts.append(jnp.where(inside[0:th, :], rolled, 0.0)[:, 0:128])
    parts.append(jnp.zeros((256 - basis * th, 128), F32))
    vertical = jnp.concatenate(parts, axis=0).T
    u_s[...] = vertical[0:th, 0 : basis * th].astype(BF16)
    for k in range(basis):
        rows = jnp.broadcast_to(taps_s[k : k + 1, :], (cols, cols))
        rolled = pltpu.roll(rows, 0, 1, stride=1, stride_axis=0)
        v_s[k] = jnp.where(inside, rolled, 0.0).astype(BF16)
    copies[1].wait()
    for k in range(basis):
        choose = (iota((basis, cols), 0) == k).astype(F32).astype(BF16)
        c_s[k] = lax.dot_general(coef_ref[...], choose, TN, preferred_element_type=F32)
    for i in range(4, 10):
        copies[i].wait()
    write_details(out_s, *held[4:])
    last = pltpu.make_async_copy(out_s.at[n], sent_ref.at[n], out_sems.at[n // group])
    last.start()
    copies[0].wait()

    def block(g):
        return pltpu.make_async_copy(
            out_s.at[pl.ds(g * group, group)], sent_ref.at[pl.ds(g * group, group)], out_sems.at[g]
        )

    def two_groups(i, carry):
        for u in range(2):
            g = 2 * i + u
            start = pl.multiple_of(g * 256, 256)
            pixels = tiles_ref[pl.ds(start, 256), :]
            for k in range(basis):
                across = jnp.dot(pixels, v_s[k], preferred_element_type=F32)
                for t in range(group):
                    coef = c_s[k, pl.ds(g * group + t, 1), :]
                    part = across[t * th : (t + 1) * th] * coef
                    a_s[u, t, k * th : (k + 1) * th, :] = part.astype(BF16)
        for u in range(2):
            g = 2 * i + u
            for t in range(group):
                done = jnp.dot(u_s[...], a_s[u, t], preferred_element_type=F32)
                out_s[g * group + t] = done.astype(BF16)
            block(g).start()
        return carry

    lax.fori_loop(0, n // group // 2, two_groups, 0)
    for g in range(n // group):
        block(g).wait()
    last.wait()


def place_strips(me_ref, strips, sender, canvas, words_s, words, sem):
    core = me_ref[0] & 1
    first = 2 * (me_ref[0] - core)
    n = strips.shape[0] - 1
    th = strips.shape[1]
    rows = 2 * th
    total = canvas.shape[0] - 1
    depth = total // 8

    def place_of(patch):
        q = patch >> 1
        x, z = (q + core) & 3, ((q >> 2) + core) & (2 * depth - 1)
        pair = x >> 1
        member = (z & 1) * 2 + ((x ^ pair) & 1)
        return jnp.where((patch & 1) == core, (member * 2 + pair) * depth + (z >> 1), total)

    lane = iota((n, 256), 1)
    details = strips[n, 0:8, 0:128].astype(F32)[:, 0:n]
    patch, offset, patch_s = (details[r : r + 1].astype(I32) for r in (0, 1, 3))
    weight, row_s, rank_s = (details[r : r + 1] for r in (2, 4, 5))
    at = place_of(patch)
    words_s[0:1, 0:n] = at
    words_s[1:2, 0:n] = offset
    words_s[2:3, 0:n] = (weight * 256.0).astype(I32)
    copy = pltpu.make_async_copy(words_s, words, sem)
    copy.start()
    off_col = as_column(offset)
    covered = (lane >= off_col) & (lane < off_col + th)
    covers = jnp.where(covered, as_column(weight), 0.0)[:, 0:128].astype(BF16)
    here = (iota((total, n), 0) == at).astype(F32).astype(BF16)
    coverage = jnp.dot(here, covers, preferred_element_type=F32)
    slot = rank_s.astype(I32) + (first + 2 * sender)
    asks = jnp.where(lane == as_column(slot), as_column(row_s), 0.0).astype(BF16)
    there = (iota((total, n), 0) == place_of(patch_s)).astype(F32).astype(BF16)
    requests = jnp.dot(there, asks, preferred_element_type=F32)

    def add_extras():
        for r, value in ((0, coverage), (1, requests[:, 0:128]), (2, requests[:, 128:256])):
            canvas[0:total, 2 * rows + r, :] = value

    def add_strips():
        copy.wait()

        def one(t, carry):
            at = words[0, t]
            off = words[1, t]
            w = words[2, t].astype(F32) * (1.0 / 256.0)
            strip = strips[t].astype(F32) * w
            for h in range(strip.shape[1] // 128):
                canvas[at, pl.ds(h * rows + off, th), :] += strip[:, h * 128 : (h + 1) * 128]
            return carry

        lax.fori_loop(0, n, one, 0, unroll=4)

    return add_extras, add_strips


def place_own_kernel(me_ref, m_ref, canvas, words_s, words, sem):
    add_extras, add_strips = place_strips(me_ref, m_ref, me_ref[0] & 1, canvas, words_s, words, sem)
    canvas[...] = jnp.zeros(canvas.shape, F32)
    add_extras()
    add_strips()


def place_other_kernel(me_ref, o_ref, own_ref, out_ref, canvas, words_s, words, sem):
    add_extras, add_strips = place_strips(me_ref, o_ref, 1 - (me_ref[0] & 1), canvas, words_s, words, sem)
    canvas[...] = jnp.zeros(canvas.shape, F32)
    add_extras()
    add_strips()
    total = out_ref.shape[0]
    out_ref[...] = (own_ref[0:total] + canvas[0:total]).astype(BF16)


def split_kernel(me_ref, parts_ref, keep_ref, send_ref):
    pair = (((me_ref[0] >> 1) + (me_ref[0] & 1)) & 3) >> 1
    members = range(parts_ref.shape[0])
    send_ref[...] = sum(parts_ref[s, 1 - pair].astype(F32) for s in members).astype(BF16)
    keep_ref[...] = sum(parts_ref[s, pair].astype(F32) for s in members)


def add_kernel(keep_ref, got_ref, out_ref):
    out_ref[...] = (keep_ref[...] + got_ref[...].astype(F32)).astype(BF16)


def coadd_kernel(parts_ref, gain_ref, out_ref, scaled_ref, asked_ref):
    rows, cols = out_ref.shape
    summed = jnp.sum(parts_ref[...].astype(F32), axis=0)
    column = as_column(jnp.maximum(summed[2 * rows : 2 * rows + 1, 0:rows], 1.0))
    for h in range(cols // 128):
        part = slice(h * 128, (h + 1) * 128)
        coadded = summed[h * rows : (h + 1) * rows] / column
        out_ref[:, part] = coadded
        for b in range(scaled_ref.shape[0]):
            scaled_ref[b, :, part] = (gain_ref[0] * coadded).astype(BF16)
        asked_ref[:, part] = summed[2 * rows + 1 + h : 2 * rows + 2 + h]


def detect_kernel(bands_ref, asked_ref, det_ref, rows_ref):
    detection = jnp.sum(bands_ref[...].astype(F32), axis=0)
    det_ref[...] = detection
    rows = det_ref.shape[0]
    ids = iota((rows, asked_ref.shape[1]), 0).astype(F32)
    hot = (ids == asked_ref[...]).astype(F32).astype(BF16)
    picked = lax.dot_general(hot, detection.astype(BF16), TN, preferred_element_type=F32)
    rows_ref[...] = picked.astype(BF16)


def flux_kernel(rows_ref, prof_ref, sp_ref, out_ref):
    patch = sp_ref[...]
    slot = 2 * patch + ranks(patch)
    each = lax.dot_general(rows_ref[...], prof_ref[...], NT, preferred_element_type=F32)
    wanted = iota(each.shape, 0) == slot
    out_ref[...] = jnp.sum(jnp.where(wanted, each, 0.0), axis=0, keepdims=True)


VM = pl.BlockSpec(memory_space=pltpu.VMEM)
SM = pl.BlockSpec(memory_space=pltpu.SMEM)
SDS = jax.ShapeDtypeStruct


def grant(mib):
    return pltpu.CompilerParams(vmem_limit_bytes=mib << 20)


def exchange(value, groups=None, axis="sky"):
    return lax.all_to_all(value, axis, split_axis=0, concat_axis=0, tiled=True, axis_index_groups=groups)


def per_device(
    tiles, coefs, tile_patch, tile_offset, weight_index, weight_table,
    taps_rows, taps_cols, gains, profiles, source_patch, source_row,
):
    sky = lax.axis_size("sky")
    band = lax.axis_size("band")
    _, n, th, cols = tiles.shape
    rows = 2 * th
    high = rows * (cols // 128) + 8
    basis = coefs.shape[2]
    depth = sky // 16
    sky_of = lambda z, x, c: (z * 4 + x) * 2 + c
    device = lambda c, x, z: sky_of((z - c) % (2 * depth), (x - c) % 4, c)
    spots = [(c, m) for c in range(2) for m in range(depth)]
    near = [
        [device(c, (3 * g) ^ e, 2 * m + b) for b in range(2) for e in range(2)] for c, m in spots for g in range(2)
    ]
    cross = [(device(c, x, z), device(c, 3 - x, z)) for c in range(2) for x in range(4) for z in range(2 * depth)]
    far = [
        [device(c, x, 2 * m + b) for m in range(depth)] for c in range(2) for b in range(2) for x in range(4)
    ]
    partners = [(i, i ^ 1) for i in range(sky)]
    me = lax.axis_index("sky").astype(I32)[None]

    inputs = (
        tiles.reshape(n * th, cols), coefs[0].T, taps_rows[0], taps_cols[0],
        tile_patch[:, :, 0], tile_offset, weight_index, weight_table, source_patch[:, :, 0], source_row,
    )
    matched = pl.pallas_call(
        match_kernel,
        out_shape=SDS((n + 1, th, cols), BF16),
        in_specs=[pl.BlockSpec(memory_space=pltpu.HBM)] * 10,
        out_specs=pl.BlockSpec(memory_space=pltpu.HBM),
        scratch_shapes=[
            pltpu.VMEM((16, cols), F32),
            pltpu.VMEM((basis, cols, cols), BF16),
            pltpu.VMEM((th, basis * th), BF16),
            pltpu.VMEM((basis, n, cols), F32),
            pltpu.VMEM((2, 256 // th, basis * th, cols), BF16),
            pltpu.VMEM((n + 1, th, cols), BF16),
        ]
        + [pltpu.VMEM(v.shape, v.dtype) for v in inputs]
        + [pltpu.SemaphoreType.DMA((len(inputs),)), pltpu.SemaphoreType.DMA((n * th // 256 + 1,))],
        name="match",
        compiler_params=grant(63),
    )(*inputs)
    other = lax.ppermute(matched, "sky", partners)

    place_scratch = [pltpu.VMEM((8, 128), I32), pltpu.SMEM((8, 128), I32), pltpu.SemaphoreType.DMA]
    own = pl.pallas_call(
        place_own_kernel,
        out_shape=SDS((sky // 2 + 1, high, 128), F32),
        in_specs=[SM, VM],
        out_specs=VM,
        scratch_shapes=place_scratch,
        name="place_own",
        compiler_params=grant(4),
    )(me, matched)
    canvas = pl.pallas_call(
        place_other_kernel,
        out_shape=SDS((sky // 2, high, 128), BF16),
        in_specs=[SM, VM, VM],
        out_specs=VM,
        scratch_shapes=[pltpu.VMEM(own.shape, F32)] + place_scratch,
        name="place_other",
        compiler_params=grant(10),
    )(me, other, own)

    along_x = exchange(canvas, near).reshape(4, 2, depth, high, 128)
    keep, send = pl.pallas_call(
        split_kernel,
        out_shape=(SDS((depth, high, 128), F32), SDS((depth, high, 128), BF16)),
        in_specs=[SM, VM],
        out_specs=(VM, VM),
        name="split",
        compiler_params=grant(8),
    )(me, along_x)
    partial = pl.pallas_call(
        add_kernel,
        out_shape=SDS((depth, high, 128), BF16),
        in_specs=[VM, VM],
        out_specs=VM,
        name="add",
        compiler_params=grant(8),
    )(keep, lax.ppermute(send, "sky", cross))
    along_z = exchange(partial, far)

    coadded, scaled, asked = pl.pallas_call(
        coadd_kernel,
        out_shape=(SDS((rows, cols), F32), SDS((band, rows, cols), BF16), SDS((1, cols), F32)),
        in_specs=[VM, SM],
        out_specs=(VM, VM, VM),
        name="coadd",
        compiler_params=grant(4),
    )(along_z, gains)
    bands = exchange(scaled, None, "band")
    detection, picked = pl.pallas_call(
        detect_kernel,
        out_shape=(SDS((rows, cols), F32), SDS((2 * sky, cols), BF16)),
        in_specs=[VM, VM],
        out_specs=(VM, VM),
        name="detect",
        compiler_params=grant(4),
    )(bands, asked)
    returned = exchange(picked.reshape(sky, 2, cols)).reshape(2 * sky, cols)
    fluxes = pl.pallas_call(
        flux_kernel,
        out_shape=SDS((1, profiles.shape[1]), F32),
        in_specs=[VM, VM, VM],
        out_specs=VM,
        name="flux",
        compiler_params=grant(4),
    )(returned, profiles[0], source_patch[:, :, 0])
    return coadded[None], detection, fluxes


def solution(mesh):
    return jax.shard_map(
        per_device,
        mesh=mesh,
        in_specs=(
            P("band", "sky", None, None),
            P("band", "sky", None),
            P("band", "sky", None),
            P("band", "sky"),
            P("band", "sky"),
            P("band", None),
            P("band", None, None),
            P("band", None, None),
            P("band"),
            P("band", "sky", None),
            P("band", "sky", None),
            P("band", "sky"),
        ),
        out_specs=(P("band", "sky", None), P("sky", None), P("band", "sky")),
        check_vma=False,
    )
```

```python
import jax
import jax.numpy as jnp
from jax import lax
from jax.experimental import pallas as pl
from jax.experimental.pallas import tpu as pltpu
from jax.sharding import PartitionSpec as P

F32 = jnp.float32
BF16 = jnp.bfloat16
I32 = jnp.int32
NT = (((1,), (1,)), ((), ()))
TN = (((0,), (0,)), ((), ()))


def iota(shape, dim):
    return lax.broadcasted_iota(I32, shape, dim)


def as_column(row):
    n = row.shape[1]
    eye = iota((n, n), 0) == iota((n, n), 1)
    return jnp.sum(jnp.where(eye, jnp.broadcast_to(row, (n, n)), jnp.zeros_like(row)), axis=1, keepdims=True)


def ranks(patch):
    n = patch.shape[1]
    column = as_column(patch)
    same = (column == patch) & (iota((n, n), 0) < iota((n, n), 1))
    return jnp.sum(same.astype(I32), axis=0, keepdims=True)


def write_details(out_ref, tp_ref, to_ref, wi_ref, wt_ref, sp_ref, sr_ref):
    n = tp_ref.shape[1]
    visits = wt_ref.shape[1]
    table = as_column(wt_ref[...].astype(F32))
    weight = jnp.sum(jnp.where(iota((visits, n), 0) == wi_ref[...], table, 0.0), axis=0, keepdims=True)
    rows = [tp_ref[...].astype(F32), to_ref[...].astype(F32), weight]
    rows += [sp_ref[...].astype(F32), sr_ref[...].astype(F32), ranks(sp_ref[...]).astype(F32)]
    rows.append(jnp.zeros((8 - len(rows), n), F32))
    block = jnp.concatenate(rows, axis=0).astype(BF16)
    out_ref[out_ref.shape[0] - 1, 0:8, 0:128] = jnp.concatenate([block, jnp.zeros((8, 128 - n), BF16)], axis=1)


def match_kernel(*refs):
    sources, sent_ref, scratch = refs[:10], refs[10], refs[11:]
    taps_s, v_s, u_s, c_s, a_s, out_s = scratch[:6]
    held, sems, out_sems = scratch[6:16], scratch[16], scratch[17]
    tiles_ref, coef_ref, tr_ref, tc_ref = held[:4]
    copies = [pltpu.make_async_copy(src, dst, sems.at[i]) for i, (src, dst) in enumerate(zip(sources, held))]
    for i in (3, 2, 1, 0, 4, 5, 6, 7, 8, 9):
        copies[i].start()

    basis, tap_total = tc_ref.shape
    half = (tap_total - 1) // 2
    cols = tiles_ref.shape[1]
    th = out_s.shape[1]
    n = coef_ref.shape[1]
    group = 256 // th
    taps_s[...] = jnp.zeros(taps_s.shape, F32)
    lag = iota((cols, cols), 1) - iota((cols, cols), 0)
    inside = (lag >= -half) & (lag <= half)
    copies[3].wait()
    copies[2].wait()
    taps_s[0:basis, 0:tap_total] = tc_ref[...].astype(F32)
    taps_s[8 : 8 + basis, 0:tap_total] = tr_ref[...].astype(F32)
    taps_s[...] = pltpu.roll(taps_s[...], cols - half, 1)
    parts = []
    for k in range(basis):
        rows = jnp.broadcast_to(taps_s[8 + k : 9 + k, :], (th, cols))
        rolled = pltpu.roll(rows, 0, 1, stride=1, stride_axis=0)
        parts.append(jnp.where(inside[0:th, :], rolled, 0.0)[:, 0:128])
    parts.append(jnp.zeros((256 - basis * th, 128), F32))
    vertical = jnp.concatenate(parts, axis=0).T
    u_s[...] = vertical[0:th, 0 : basis * th].astype(BF16)
    for k in range(basis):
        rows = jnp.broadcast_to(taps_s[k : k + 1, :], (cols, cols))
        rolled = pltpu.roll(rows, 0, 1, stride=1, stride_axis=0)
        v_s[k] = jnp.where(inside, rolled, 0.0).astype(BF16)
    copies[1].wait()
    for k in range(basis):
        choose = (iota((basis, cols), 0) == k).astype(F32).astype(BF16)
        c_s[k] = lax.dot_general(coef_ref[...], choose, TN, preferred_element_type=F32)
    for i in range(4, 10):
        copies[i].wait()
    write_details(out_s, *held[4:])
    last = pltpu.make_async_copy(out_s.at[n], sent_ref.at[n], out_sems.at[n // group])
    last.start()
    copies[0].wait()

    def block(g):
        return pltpu.make_async_copy(
            out_s.at[pl.ds(g * group, group)], sent_ref.at[pl.ds(g * group, group)], out_sems.at[g]
        )

    def two_groups(i, carry):
        for u in range(2):
            g = 2 * i + u
            start = pl.multiple_of(g * 256, 256)
            pixels = tiles_ref[pl.ds(start, 256), :]
            for k in range(basis):
                across = jnp.dot(pixels, v_s[k], preferred_element_type=F32)
                for t in range(group):
                    coef = c_s[k, pl.ds(g * group + t, 1), :]
                    part = across[t * th : (t + 1) * th] * coef
                    a_s[u, t, k * th : (k + 1) * th, :] = part.astype(BF16)
        for u in range(2):
            g = 2 * i + u
            for t in range(group):
                done = jnp.dot(u_s[...], a_s[u, t], preferred_element_type=F32)
                out_s[g * group + t] = done.astype(BF16)
            block(g).start()
        return carry

    lax.fori_loop(0, n // group // 2, two_groups, 0)
    for g in range(n // group):
        block(g).wait()
    last.wait()


def place_strips(me_ref, strips, sender, canvas, words_s, words, sem):
    core = me_ref[0] & 1
    first = 2 * (me_ref[0] - core)
    n = strips.shape[0] - 1
    th = strips.shape[1]
    rows = 2 * th
    total = canvas.shape[0] - 1
    depth = total // 8

    def place_of(patch):
        q = patch >> 1
        x, z = (q + core) & 3, q >> 2
        pair = x >> 1
        member = ((z + core) & 1) * 2 + ((x ^ pair) & 1)
        return jnp.where((patch & 1) == core, (member * 2 + pair) * depth + (z >> 1), total)

    lane = iota((n, 256), 1)
    details = strips[n, 0:8, 0:128].astype(F32)[:, 0:n]
    patch, offset, patch_s = (details[r : r + 1].astype(I32) for r in (0, 1, 3))
    weight, row_s, rank_s = (details[r : r + 1] for r in (2, 4, 5))
    at = place_of(patch)
    words_s[0:1, 0:n] = at
    words_s[1:2, 0:n] = offset
    words_s[2:3, 0:n] = (weight * 256.0).astype(I32)
    copy = pltpu.make_async_copy(words_s, words, sem)
    copy.start()
    off_col = as_column(offset)
    covered = (lane >= off_col) & (lane < off_col + th)
    covers = jnp.where(covered, as_column(weight), 0.0)[:, 0:128].astype(BF16)
    here = (iota((total, n), 0) == at).astype(F32).astype(BF16)
    coverage = jnp.dot(here, covers, preferred_element_type=F32)
    slot = rank_s.astype(I32) + (first + 2 * sender)
    asks = jnp.where(lane == as_column(slot), as_column(row_s), 0.0).astype(BF16)
    there = (iota((total, n), 0) == place_of(patch_s)).astype(F32).astype(BF16)
    requests = jnp.dot(there, asks, preferred_element_type=F32)

    def add_extras():
        for r, value in ((0, coverage), (1, requests[:, 0:128]), (2, requests[:, 128:256])):
            canvas[0:total, 2 * rows + r, :] = value

    def add_strips():
        copy.wait()

        def one(t, carry):
            at = words[0, t]
            off = words[1, t]
            w = words[2, t].astype(F32) * (1.0 / 256.0)
            strip = strips[t].astype(F32) * w
            for h in range(strip.shape[1] // 128):
                canvas[at, pl.ds(h * rows + off, th), :] += strip[:, h * 128 : (h + 1) * 128]
            return carry

        lax.fori_loop(0, n, one, 0, unroll=4)

    return add_extras, add_strips


def place_own_kernel(me_ref, m_ref, canvas, words_s, words, sem):
    add_extras, add_strips = place_strips(me_ref, m_ref, me_ref[0] & 1, canvas, words_s, words, sem)
    canvas[...] = jnp.zeros(canvas.shape, F32)
    add_extras()
    add_strips()


def place_other_kernel(me_ref, o_ref, own_ref, out_ref, canvas, words_s, words, sem):
    add_extras, add_strips = place_strips(me_ref, o_ref, 1 - (me_ref[0] & 1), canvas, words_s, words, sem)
    canvas[...] = jnp.zeros(canvas.shape, F32)
    add_extras()
    add_strips()
    total = out_ref.shape[0]
    out_ref[...] = (own_ref[0:total] + canvas[0:total]).astype(BF16)


def split_kernel(me_ref, parts_ref, keep_ref, send_ref):
    pair = (((me_ref[0] >> 1) + (me_ref[0] & 1)) & 3) >> 1
    members = range(parts_ref.shape[0])
    send_ref[...] = sum(parts_ref[s, 1 - pair].astype(F32) for s in members).astype(BF16)
    keep_ref[...] = sum(parts_ref[s, pair].astype(F32) for s in members)


def add_kernel(keep_ref, got_ref, out_ref):
    out_ref[...] = (keep_ref[...] + got_ref[...].astype(F32)).astype(BF16)


def coadd_kernel(parts_ref, gain_ref, out_ref, scaled_ref, asked_ref):
    rows, cols = out_ref.shape
    summed = jnp.sum(parts_ref[...].astype(F32), axis=0)
    column = as_column(jnp.maximum(summed[2 * rows : 2 * rows + 1, 0:rows], 1.0))
    for h in range(cols // 128):
        part = slice(h * 128, (h + 1) * 128)
        coadded = summed[h * rows : (h + 1) * rows] / column
        out_ref[:, part] = coadded
        for b in range(scaled_ref.shape[0]):
            scaled_ref[b, :, part] = (gain_ref[0] * coadded).astype(BF16)
        asked_ref[:, part] = summed[2 * rows + 1 + h : 2 * rows + 2 + h]


def detect_kernel(bands_ref, asked_ref, det_ref, rows_ref):
    detection = jnp.sum(bands_ref[...].astype(F32), axis=0)
    det_ref[...] = detection
    rows = det_ref.shape[0]
    ids = iota((rows, asked_ref.shape[1]), 0).astype(F32)
    hot = (ids == asked_ref[...]).astype(F32).astype(BF16)
    picked = lax.dot_general(hot, detection.astype(BF16), TN, preferred_element_type=F32)
    rows_ref[...] = picked.astype(BF16)


def flux_kernel(rows_ref, prof_ref, sp_ref, out_ref):
    patch = sp_ref[...]
    slot = 2 * patch + ranks(patch)
    each = lax.dot_general(rows_ref[...], prof_ref[...], NT, preferred_element_type=F32)
    wanted = iota(each.shape, 0) == slot
    out_ref[...] = jnp.sum(jnp.where(wanted, each, 0.0), axis=0, keepdims=True)


VM = pl.BlockSpec(memory_space=pltpu.VMEM)
SM = pl.BlockSpec(memory_space=pltpu.SMEM)
SDS = jax.ShapeDtypeStruct


def grant(mib):
    return pltpu.CompilerParams(vmem_limit_bytes=mib << 20)


def exchange(value, groups=None, axis="sky"):
    return lax.all_to_all(value, axis, split_axis=0, concat_axis=0, tiled=True, axis_index_groups=groups)


def per_device(
    tiles, coefs, tile_patch, tile_offset, weight_index, weight_table,
    taps_rows, taps_cols, gains, profiles, source_patch, source_row,
):
    sky = lax.axis_size("sky")
    band = lax.axis_size("band")
    _, n, th, cols = tiles.shape
    rows = 2 * th
    high = rows * (cols // 128) + 8
    basis = coefs.shape[2]
    depth = sky // 16
    sky_of = lambda z, x, c: (z * 4 + x) * 2 + c
    device = lambda c, x, z: sky_of((z - c) % (2 * depth), (x - c) % 4, c)
    spots = [(c, m) for c in range(2) for m in range(depth)]
    near = [
        [device(c, (3 * g) ^ e, 2 * m + b) for b in range(2) for e in range(2)] for c, m in spots for g in range(2)
    ]
    cross = [(device(c, x, z), device(c, 3 - x, z)) for c in range(2) for x in range(4) for z in range(2 * depth)]
    far = [[sky_of(2 * m + b, x, c) for m in range(depth)] for b in range(2) for x in range(4) for c in range(2)]
    partners = [(i, i ^ 1) for i in range(sky)]
    me = lax.axis_index("sky").astype(I32)[None]

    inputs = (
        tiles.reshape(n * th, cols), coefs[0].T, taps_rows[0], taps_cols[0],
        tile_patch[:, :, 0], tile_offset, weight_index, weight_table, source_patch[:, :, 0], source_row,
    )
    matched = pl.pallas_call(
        match_kernel,
        out_shape=SDS((n + 1, th, cols), BF16),
        in_specs=[pl.BlockSpec(memory_space=pltpu.HBM)] * 10,
        out_specs=pl.BlockSpec(memory_space=pltpu.HBM),
        scratch_shapes=[
            pltpu.VMEM((16, cols), F32),
            pltpu.VMEM((basis, cols, cols), BF16),
            pltpu.VMEM((th, basis * th), BF16),
            pltpu.VMEM((basis, n, cols), F32),
            pltpu.VMEM((2, 256 // th, basis * th, cols), BF16),
            pltpu.VMEM((n + 1, th, cols), BF16),
        ]
        + [pltpu.VMEM(v.shape, v.dtype) for v in inputs]
        + [pltpu.SemaphoreType.DMA((len(inputs),)), pltpu.SemaphoreType.DMA((n * th // 256 + 1,))],
        name="match",
        compiler_params=grant(63),
    )(*inputs)
    other = lax.ppermute(matched, "sky", partners)

    place_scratch = [pltpu.VMEM((8, 128), I32), pltpu.SMEM((8, 128), I32), pltpu.SemaphoreType.DMA]
    own = pl.pallas_call(
        place_own_kernel,
        out_shape=SDS((sky // 2 + 1, high, 128), F32),
        in_specs=[SM, VM],
        out_specs=VM,
        scratch_shapes=place_scratch,
        name="place_own",
        compiler_params=grant(4),
    )(me, matched)
    canvas = pl.pallas_call(
        place_other_kernel,
        out_shape=SDS((sky // 2, high, 128), BF16),
        in_specs=[SM, VM, VM],
        out_specs=VM,
        scratch_shapes=[pltpu.VMEM(own.shape, F32)] + place_scratch,
        name="place_other",
        compiler_params=grant(10),
    )(me, other, own)

    along_x = exchange(canvas, near).reshape(4, 2, depth, high, 128)
    keep, send = pl.pallas_call(
        split_kernel,
        out_shape=(SDS((depth, high, 128), F32), SDS((depth, high, 128), BF16)),
        in_specs=[SM, VM],
        out_specs=(VM, VM),
        name="split",
        compiler_params=grant(8),
    )(me, along_x)
    partial = pl.pallas_call(
        add_kernel,
        out_shape=SDS((depth, high, 128), BF16),
        in_specs=[VM, VM],
        out_specs=VM,
        name="add",
        compiler_params=grant(8),
    )(keep, lax.ppermute(send, "sky", cross))
    along_z = exchange(partial, far)

    coadded, scaled, asked = pl.pallas_call(
        coadd_kernel,
        out_shape=(SDS((rows, cols), F32), SDS((band, rows, cols), BF16), SDS((1, cols), F32)),
        in_specs=[VM, SM],
        out_specs=(VM, VM, VM),
        name="coadd",
        compiler_params=grant(4),
    )(along_z, gains)
    bands = exchange(scaled, None, "band")
    detection, picked = pl.pallas_call(
        detect_kernel,
        out_shape=(SDS((rows, cols), F32), SDS((2 * sky, cols), BF16)),
        in_specs=[VM, VM],
        out_specs=(VM, VM),
        name="detect",
        compiler_params=grant(4),
    )(bands, asked)
    returned = exchange(picked.reshape(sky, 2, cols)).reshape(2 * sky, cols)
    fluxes = pl.pallas_call(
        flux_kernel,
        out_shape=SDS((1, profiles.shape[1]), F32),
        in_specs=[VM, VM, VM],
        out_specs=VM,
        name="flux",
        compiler_params=grant(4),
    )(returned, profiles[0], source_patch[:, :, 0])
    return coadded[None], detection, fluxes


def solution(mesh):
    return jax.shard_map(
        per_device,
        mesh=mesh,
        in_specs=(
            P("band", "sky", None, None),
            P("band", "sky", None),
            P("band", "sky", None),
            P("band", "sky"),
            P("band", "sky"),
            P("band", None),
            P("band", None, None),
            P("band", None, None),
            P("band"),
            P("band", "sky", None),
            P("band", "sky", None),
            P("band", "sky"),
        ),
        out_specs=(P("band", "sky", None), P("sky", None), P("band", "sky")),
        check_vma=False,
    )
```

```python
import jax
import jax.numpy as jnp
from jax import lax
from jax.experimental import pallas as pl
from jax.experimental.pallas import tpu as pltpu
from jax.sharding import PartitionSpec as P

F32 = jnp.float32
BF16 = jnp.bfloat16
I32 = jnp.int32
NT = (((1,), (1,)), ((), ()))
TN = (((0,), (0,)), ((), ()))


def iota(shape, dim):
    return lax.broadcasted_iota(I32, shape, dim)


def as_column(row):
    n = row.shape[1]
    eye = iota((n, n), 0) == iota((n, n), 1)
    return jnp.sum(jnp.where(eye, jnp.broadcast_to(row, (n, n)), jnp.zeros_like(row)), axis=1, keepdims=True)


def ranks(patch):
    n = patch.shape[1]
    column = as_column(patch)
    same = (column == patch) & (iota((n, n), 0) < iota((n, n), 1))
    return jnp.sum(same.astype(I32), axis=0, keepdims=True)


def write_details(out_ref, tp_ref, to_ref, wi_ref, wt_ref, sp_ref, sr_ref):
    n = tp_ref.shape[1]
    visits = wt_ref.shape[1]
    table = as_column(wt_ref[...].astype(F32))
    weight = jnp.sum(jnp.where(iota((visits, n), 0) == wi_ref[...], table, 0.0), axis=0, keepdims=True)
    rows = [tp_ref[...].astype(F32), to_ref[...].astype(F32), weight]
    rows += [sp_ref[...].astype(F32), sr_ref[...].astype(F32), ranks(sp_ref[...]).astype(F32)]
    rows.append(jnp.zeros((8 - len(rows), n), F32))
    block = jnp.concatenate(rows, axis=0).astype(BF16)
    out_ref[out_ref.shape[0] - 1, 0:8, 0:128] = jnp.concatenate([block, jnp.zeros((8, 128 - n), BF16)], axis=1)


def match_kernel(*refs):
    sources, sent_ref, scratch = refs[:10], refs[10], refs[11:]
    taps_s, v_s, u_s, c_s, a_s, out_s = scratch[:6]
    held, sems, out_sems = scratch[6:16], scratch[16], scratch[17]
    tiles_ref, coef_ref, tr_ref, tc_ref = held[:4]
    copies = [pltpu.make_async_copy(src, dst, sems.at[i]) for i, (src, dst) in enumerate(zip(sources, held))]
    for i in (3, 2, 1, 0, 4, 5, 6, 7, 8, 9):
        copies[i].start()

    basis, tap_total = tc_ref.shape
    half = (tap_total - 1) // 2
    cols = tiles_ref.shape[1]
    th = out_s.shape[1]
    n = coef_ref.shape[1]
    group = 256 // th
    taps_s[...] = jnp.zeros(taps_s.shape, F32)
    lag = iota((cols, cols), 1) - iota((cols, cols), 0)
    inside = (lag >= -half) & (lag <= half)
    copies[3].wait()
    copies[2].wait()
    taps_s[0:basis, 0:tap_total] = tc_ref[...].astype(F32)
    taps_s[8 : 8 + basis, 0:tap_total] = tr_ref[...].astype(F32)
    taps_s[...] = pltpu.roll(taps_s[...], cols - half, 1)
    parts = []
    for k in range(basis):
        rows = jnp.broadcast_to(taps_s[8 + k : 9 + k, :], (th, cols))
        rolled = pltpu.roll(rows, 0, 1, stride=1, stride_axis=0)
        parts.append(jnp.where(inside[0:th, :], rolled, 0.0)[:, 0:128])
    parts.append(jnp.zeros((256 - basis * th, 128), F32))
    vertical = jnp.concatenate(parts, axis=0).T
    u_s[...] = vertical[0:th, 0 : basis * th].astype(BF16)
    for k in range(basis):
        rows = jnp.broadcast_to(taps_s[k : k + 1, :], (cols, cols))
        rolled = pltpu.roll(rows, 0, 1, stride=1, stride_axis=0)
        v_s[k] = jnp.where(inside, rolled, 0.0).astype(BF16)
    copies[1].wait()
    for k in range(basis):
        choose = (iota((basis, cols), 0) == k).astype(F32).astype(BF16)
        c_s[k] = lax.dot_general(coef_ref[...], choose, TN, preferred_element_type=F32)
    for i in range(4, 10):
        copies[i].wait()
    write_details(out_s, *held[4:])
    last = pltpu.make_async_copy(out_s.at[n], sent_ref.at[n], out_sems.at[n // group])
    last.start()
    copies[0].wait()

    def block(g):
        return pltpu.make_async_copy(
            out_s.at[pl.ds(g * group, group)], sent_ref.at[pl.ds(g * group, group)], out_sems.at[g]
        )

    def two_groups(i, carry):
        for u in range(2):
            g = 2 * i + u
            start = pl.multiple_of(g * 256, 256)
            pixels = tiles_ref[pl.ds(start, 256), :]
            for k in range(basis):
                across = jnp.dot(pixels, v_s[k], preferred_element_type=F32)
                for t in range(group):
                    coef = c_s[k, pl.ds(g * group + t, 1), :]
                    part = across[t * th : (t + 1) * th] * coef
                    a_s[u, t, k * th : (k + 1) * th, :] = part.astype(BF16)
        for u in range(2):
            g = 2 * i + u
            for t in range(group):
                done = jnp.dot(u_s[...], a_s[u, t], preferred_element_type=F32)
                out_s[g * group + t] = done.astype(BF16)
            block(g).start()
        return carry

    lax.fori_loop(0, n // group // 2, two_groups, 0)
    for g in range(n // group):
        block(g).wait()
    last.wait()


def place_strips(me_ref, strips, sender, canvas, words_s, words, sem):
    core = me_ref[0] & 1
    first = 2 * (me_ref[0] - core)
    n = strips.shape[0] - 1
    th = strips.shape[1]
    rows = 2 * th
    total = canvas.shape[0] - 1
    depth = total // 8

    def place_of(patch):
        q = patch >> 1
        x, z = (q + core) & 3, q >> 2
        pair = x >> 1
        member = ((z + core) & 1) * 2 + ((x ^ pair) & 1)
        return jnp.where((patch & 1) == core, (member * 2 + pair) * depth + (z >> 1), total)

    lane = iota((n, 256), 1)
    details = strips[n, 0:8, 0:128].astype(F32)[:, 0:n]
    patch, offset, patch_s = (details[r : r + 1].astype(I32) for r in (0, 1, 3))
    weight, row_s, rank_s = (details[r : r + 1] for r in (2, 4, 5))
    at = place_of(patch)
    words_s[0:1, 0:n] = at
    words_s[1:2, 0:n] = offset
    words_s[2:3, 0:n] = (weight * 256.0).astype(I32)
    copy = pltpu.make_async_copy(words_s, words, sem)
    copy.start()
    off_col = as_column(offset)
    covered = (lane >= off_col) & (lane < off_col + th)
    covers = jnp.where(covered, as_column(weight), 0.0)[:, 0:128].astype(BF16)
    here = (iota((total, n), 0) == at).astype(F32).astype(BF16)
    coverage = jnp.dot(here, covers, preferred_element_type=F32)
    slot = rank_s.astype(I32) + (first + 2 * sender)
    asks = jnp.where(lane == as_column(slot), as_column(row_s), 0.0).astype(BF16)
    there = (iota((total, n), 0) == place_of(patch_s)).astype(F32).astype(BF16)
    requests = jnp.dot(there, asks, preferred_element_type=F32)

    def add_extras():
        for r, value in ((0, coverage), (1, requests[:, 0:128]), (2, requests[:, 128:256])):
            canvas[0:total, 2 * rows + r, :] = value

    def add_strips():
        copy.wait()

        def one(t, carry):
            at = words[0, t]
            off = words[1, t]
            w = words[2, t].astype(F32) * (1.0 / 256.0)
            strip = strips[t].astype(F32) * w
            for h in range(strip.shape[1] // 128):
                canvas[at, pl.ds(h * rows + off, th), :] += strip[:, h * 128 : (h + 1) * 128]
            return carry

        lax.fori_loop(0, n, one, 0, unroll=4)

    return add_extras, add_strips


def place_own_kernel(me_ref, m_ref, canvas, words_s, words, sem):
    add_extras, add_strips = place_strips(me_ref, m_ref, me_ref[0] & 1, canvas, words_s, words, sem)
    canvas[...] = jnp.zeros(canvas.shape, F32)
    add_extras()
    add_strips()


def place_other_kernel(me_ref, o_ref, own_ref, out_ref, canvas, words_s, words, sem):
    add_extras, add_strips = place_strips(me_ref, o_ref, 1 - (me_ref[0] & 1), canvas, words_s, words, sem)
    canvas[...] = jnp.zeros(canvas.shape, F32)
    add_extras()
    add_strips()
    total = out_ref.shape[0]
    out_ref[...] = (own_ref[0:total] + canvas[0:total]).astype(BF16)


def split_kernel(me_ref, parts_ref, keep_ref, send_ref):
    pair = (((me_ref[0] >> 1) + (me_ref[0] & 1)) & 3) >> 1
    members = range(parts_ref.shape[0])
    send_ref[...] = sum(parts_ref[s, 1 - pair].astype(F32) for s in members).astype(BF16)
    keep_ref[...] = sum(parts_ref[s, pair].astype(F32) for s in members)


def add_kernel(gain_ref, keep_ref, got_ref, out_ref, spread_ref):
    spread_ref[...] = jnp.full(spread_ref.shape, gain_ref[0], F32)
    out_ref[...] = (keep_ref[...] + got_ref[...].astype(F32)).astype(BF16)


def coadd_kernel(parts_ref, gain_ref, out_ref, scaled_ref, asked_ref):
    rows, cols = out_ref.shape
    summed = jnp.sum(parts_ref[...].astype(F32), axis=0)
    column = as_column(jnp.maximum(summed[2 * rows : 2 * rows + 1, 0:rows], 1.0))
    for h in range(cols // 128):
        part = slice(h * 128, (h + 1) * 128)
        coadded = summed[h * rows : (h + 1) * rows] / column
        out_ref[:, part] = coadded
        for b in range(scaled_ref.shape[0]):
            scaled_ref[b, :, part] = (gain_ref[0:1, :] * coadded).astype(BF16)
        asked_ref[:, part] = summed[2 * rows + 1 + h : 2 * rows + 2 + h]


def detect_kernel(bands_ref, asked_ref, det_ref, rows_ref):
    detection = jnp.sum(bands_ref[...].astype(F32), axis=0)
    det_ref[...] = detection
    rows = det_ref.shape[0]
    ids = iota((rows, asked_ref.shape[1]), 0).astype(F32)
    hot = (ids == asked_ref[...]).astype(F32).astype(BF16)
    picked = lax.dot_general(hot, detection.astype(BF16), TN, preferred_element_type=F32)
    rows_ref[...] = picked.astype(BF16)


def flux_kernel(rows_ref, prof_ref, sp_ref, out_ref):
    patch = sp_ref[...]
    slot = 2 * patch + ranks(patch)
    each = lax.dot_general(rows_ref[...], prof_ref[...], NT, preferred_element_type=F32)
    wanted = iota(each.shape, 0) == slot
    out_ref[...] = jnp.sum(jnp.where(wanted, each, 0.0), axis=0, keepdims=True)


VM = pl.BlockSpec(memory_space=pltpu.VMEM)
SM = pl.BlockSpec(memory_space=pltpu.SMEM)
SDS = jax.ShapeDtypeStruct


def grant(mib):
    return pltpu.CompilerParams(vmem_limit_bytes=mib << 20)


def exchange(value, groups=None, axis="sky"):
    return lax.all_to_all(value, axis, split_axis=0, concat_axis=0, tiled=True, axis_index_groups=groups)


def per_device(
    tiles, coefs, tile_patch, tile_offset, weight_index, weight_table,
    taps_rows, taps_cols, gains, profiles, source_patch, source_row,
):
    sky = lax.axis_size("sky")
    band = lax.axis_size("band")
    _, n, th, cols = tiles.shape
    rows = 2 * th
    high = rows * (cols // 128) + 8
    basis = coefs.shape[2]
    depth = sky // 16
    sky_of = lambda z, x, c: (z * 4 + x) * 2 + c
    device = lambda c, x, z: sky_of((z - c) % (2 * depth), (x - c) % 4, c)
    spots = [(c, m) for c in range(2) for m in range(depth)]
    near = [
        [device(c, (3 * g) ^ e, 2 * m + b) for b in range(2) for e in range(2)] for c, m in spots for g in range(2)
    ]
    cross = [(device(c, x, z), device(c, 3 - x, z)) for c in range(2) for x in range(4) for z in range(2 * depth)]
    far = [[sky_of(2 * m + b, x, c) for m in range(depth)] for b in range(2) for x in range(4) for c in range(2)]
    partners = [(i, i ^ 1) for i in range(sky)]
    me = lax.axis_index("sky").astype(I32)[None]

    inputs = (
        tiles.reshape(n * th, cols), coefs[0].T, taps_rows[0], taps_cols[0],
        tile_patch[:, :, 0], tile_offset, weight_index, weight_table, source_patch[:, :, 0], source_row,
    )
    matched = pl.pallas_call(
        match_kernel,
        out_shape=SDS((n + 1, th, cols), BF16),
        in_specs=[pl.BlockSpec(memory_space=pltpu.HBM)] * 10,
        out_specs=pl.BlockSpec(memory_space=pltpu.HBM),
        scratch_shapes=[
            pltpu.VMEM((16, cols), F32),
            pltpu.VMEM((basis, cols, cols), BF16),
            pltpu.VMEM((th, basis * th), BF16),
            pltpu.VMEM((basis, n, cols), F32),
            pltpu.VMEM((2, 256 // th, basis * th, cols), BF16),
            pltpu.VMEM((n + 1, th, cols), BF16),
        ]
        + [pltpu.VMEM(v.shape, v.dtype) for v in inputs]
        + [pltpu.SemaphoreType.DMA((len(inputs),)), pltpu.SemaphoreType.DMA((n * th // 256 + 1,))],
        name="match",
        compiler_params=grant(63),
    )(*inputs)
    other = lax.ppermute(matched, "sky", partners)

    place_scratch = [pltpu.VMEM((8, 128), I32), pltpu.SMEM((8, 128), I32), pltpu.SemaphoreType.DMA]
    own = pl.pallas_call(
        place_own_kernel,
        out_shape=SDS((sky // 2 + 1, high, 128), F32),
        in_specs=[SM, VM],
        out_specs=VM,
        scratch_shapes=place_scratch,
        name="place_own",
        compiler_params=grant(4),
    )(me, matched)
    canvas = pl.pallas_call(
        place_other_kernel,
        out_shape=SDS((sky // 2, high, 128), BF16),
        in_specs=[SM, VM, VM],
        out_specs=VM,
        scratch_shapes=[pltpu.VMEM(own.shape, F32)] + place_scratch,
        name="place_other",
        compiler_params=grant(10),
    )(me, other, own)

    along_x = exchange(canvas, near).reshape(4, 2, depth, high, 128)
    keep, send = pl.pallas_call(
        split_kernel,
        out_shape=(SDS((depth, high, 128), F32), SDS((depth, high, 128), BF16)),
        in_specs=[SM, VM],
        out_specs=(VM, VM),
        name="split",
        compiler_params=grant(8),
    )(me, along_x)
    partial, gain = pl.pallas_call(
        add_kernel,
        out_shape=(SDS((depth, high, 128), BF16), SDS((8, 128), F32)),
        in_specs=[SM, VM, VM],
        out_specs=(VM, VM),
        name="add",
        compiler_params=grant(8),
    )(gains, keep, lax.ppermute(send, "sky", cross))
    along_z = exchange(partial, far)

    coadded, scaled, asked = pl.pallas_call(
        coadd_kernel,
        out_shape=(SDS((rows, cols), F32), SDS((band, rows, cols), BF16), SDS((1, cols), F32)),
        in_specs=[VM, VM],
        out_specs=(VM, VM, VM),
        name="coadd",
        compiler_params=grant(4),
    )(along_z, gain)
    bands = exchange(scaled, None, "band")
    detection, picked = pl.pallas_call(
        detect_kernel,
        out_shape=(SDS((rows, cols), F32), SDS((2 * sky, cols), BF16)),
        in_specs=[VM, VM],
        out_specs=(VM, VM),
        name="detect",
        compiler_params=grant(4),
    )(bands, asked)
    returned = exchange(picked.reshape(sky, 2, cols)).reshape(2 * sky, cols)
    fluxes = pl.pallas_call(
        flux_kernel,
        out_shape=SDS((1, profiles.shape[1]), F32),
        in_specs=[VM, VM, VM],
        out_specs=VM,
        name="flux",
        compiler_params=grant(4),
    )(returned, profiles[0], source_patch[:, :, 0])
    return coadded[None], detection, fluxes


def solution(mesh):
    return jax.shard_map(
        per_device,
        mesh=mesh,
        in_specs=(
            P("band", "sky", None, None),
            P("band", "sky", None),
            P("band", "sky", None),
            P("band", "sky"),
            P("band", "sky"),
            P("band", None),
            P("band", None, None),
            P("band", None, None),
            P("band"),
            P("band", "sky", None),
            P("band", "sky", None),
            P("band", "sky"),
        ),
        out_specs=(P("band", "sky", None), P("sky", None), P("band", "sky")),
        check_vma=False,
    )
```
